32 devices in a mesh: dp: 8 (over z, y), mp: 4 (over x, core).
Axes of the slice: x: 2, y: 2, z: 4, core: 2. Of those that a mesh axis runs over, the one named last changes fastest.
Arguments:
- tokens: bfloat16 [2048, 2048], P('dp'), may hold values from -6 to 6
- out_grad: bfloat16 [2048, 2048], P('dp'), may hold values from -6 to 6
- master: float32 [2368, 3, 7168], P('dp', None, 'mp'), may hold values from -6 to 6
- moment_one: float32 [2368, 3, 7168], P('dp', None, 'mp'), may hold values from -6 to 6
- moment_two: float32 [2368, 3, 7168], P('dp', None, 'mp'), may hold values from 0.05 to 5
- old_offsets: int32 [9], replicated, may hold values from 0 to 2048, as said below
- new_offsets: int32 [9], replicated, may hold values from 0 to 2048, as said below
Outputs:
- new_master: float32 [2880, 3, 7168], P('dp', None, 'mp')
- new_moment_one: float32 [2880, 3, 7168], P('dp', None, 'mp')
- new_moment_two: float32 [2880, 3, 7168], P('dp', None, 'mp')
- layer_output: bfloat16 [2048, 2048], P('dp', 'mp')
The draws below stay inside these ranges and needn't reach their ends.
Inputs may be any that keep to these rules, and one draw needn't show every extreme that they name: non-decreasing, old_offsets[0] = 0 and old_offsets[8] = 2048; device p holds rows old_offsets[p] to old_offsets[p + 1] - 1 in its first slots; every device holds at least one and at most 296 rows, and some device exactly 296. non-decreasing, new_offsets[0] = 0 and new_offsets[8] = 2048; exactly one device holds no rows, its index at least 2 and at most 3; every other device holds at least one and at most 360 rows, some device exactly 360; a row's device in the new layout is its device in the old layout or the next one along dp.
All inputs are finite; a program needn't handle non-finite values.
Results may differ from the reference program's by a relative error of at most 0.014.
Values may be sent and summed in bfloat16 or wider, within the bound.
A program may use at most 256 MiB of HBM per device.

```python
import math
import jax
import jax.numpy as jnp
from jax import lax

FEATURE_WIDTH = 2048
FF = 7168
TOK_DEV = 256
TOKENS = 2048
SHARD = 256
MAX_SHIFT = 20
CAP_OLD = 296
CAP_NEW = 360
N_DP = 8
N_MP = 4


def full_layout(key):
    base_key = jax.random.fold_in(key, 11)
    lost_key, forced_key, wiggle_key = jax.random.split(base_key, 3)
    leaving = jax.random.randint(lost_key, (), 2, N_DP // 2, dtype=jnp.int32)
    forced = jax.random.randint(forced_key, (), 2, N_DP - 2, dtype=jnp.int32)
    device_ids = jnp.arange(N_DP + 1, dtype=jnp.int32)
    wiggle = jax.random.randint(wiggle_key, (N_DP + 1,), -1, 2, dtype=jnp.int32)
    free_bound = (device_ids > 0) & (device_ids < N_DP) & (device_ids != forced) & (device_ids != forced + 1)
    old_bounds = device_ids * SHARD
    old_bounds = old_bounds + jnp.where(device_ids == forced, -MAX_SHIFT, 0)
    old_bounds = old_bounds + jnp.where(device_ids == forced + 1, MAX_SHIFT, 0)
    old_bounds = (old_bounds + jnp.where(free_bound, wiggle, 0)).astype(jnp.int32)
    old_sizes = (old_bounds[1:] - old_bounds[:-1]).astype(jnp.int32)
    lost_size = jnp.sum(jnp.where(jnp.arange(N_DP, dtype=jnp.int32) == leaving, old_sizes, 0)).astype(jnp.int32)

    def carry_step(previous, inputs):
        position, size_before = inputs
        pushed = jnp.maximum(previous + size_before - CAP_NEW, 1)
        moved_rows = jnp.where(position < leaving, 1, jnp.where(position == leaving, 0, jnp.where(position == leaving + 1, lost_size, pushed))).astype(jnp.int32)
        return (moved_rows, moved_rows)
    final_moved, inner_moves = lax.scan(carry_step, jnp.zeros((), jnp.int32), (jnp.arange(1, N_DP, dtype=jnp.int32), old_sizes[:-1]))
    boundary_moves = jnp.concatenate([jnp.zeros((1,), jnp.int32), inner_moves, jnp.zeros((1,), jnp.int32)])
    new_bounds = (old_bounds - boundary_moves).astype(jnp.int32)
    return (old_bounds, new_bounds)


def draw_new_offsets(key, part):
    old_bounds, new_bounds = full_layout(key)
    return new_bounds


def draw_old_offsets(key, part):
    old_bounds, new_bounds = full_layout(key)
    return old_bounds


def spiked(values, stream_key, source, target, blocks, factor):
    def block_of(dim):
        return (jnp.arange(values.shape[dim]) // (values.shape[dim] // blocks)).reshape((-1,) + (1,) * (values.ndim - 1 - dim))

    first = jax.random.permutation(stream_key, blocks)[block_of(target)]
    other_side = (block_of(target) + blocks // 2) % blocks
    return jnp.where((block_of(source) == first) | (block_of(source) == other_side), factor * values, values)


def level_of(own_key, shape, cuts, low, high):
    factor_of, own = 1.0, jax.random.fold_in(own_key, 6)
    for axis_at, parts in cuts:
        steps = jnp.exp(jax.random.uniform(jax.random.fold_in(own, axis_at), (parts,), jnp.float32, low / len(cuts), high / len(cuts)))
        factor_of = factor_of * jnp.repeat(steps, shape[axis_at] // parts).reshape([-1 if axis == axis_at else 1 for axis in range(len(shape))])
    return factor_of


def normal_values(key, shape, width, bound, pieces=(), kind=jnp.bfloat16):
    loudness = level_of(key, shape, pieces, -0.22, 0.18) if pieces else 1.0
    values = jax.random.normal(key, shape, jnp.float32) * width * loudness
    return jnp.minimum(jnp.maximum(values, -bound), bound).astype(kind)


def noise_with(own_key, shape, scale, limit, cuts, heavy, kind=jnp.bfloat16):
    entries = scale * jax.random.normal(own_key, shape, jnp.float32)
    if cuts:
        entries = entries * level_of(own_key, shape, cuts, -0.22, 0.18)
    return jnp.clip(spiked(entries, jax.random.fold_in(own_key, 3), *heavy), -limit, limit).astype(kind)


def setup_inputs(seed: int = 0) -> dict:
    splits = jax.random.split(jax.random.key(seed), 8)
    tokens = noise_with(splits[0], (TOKENS, FEATURE_WIDTH), 1.0, 6.0, ((0, 8),), (0, 1, 8, 2.0))
    out_grad = normal_values(splits[1], (TOKENS, FEATURE_WIDTH), 1.0, 6.0, ((0, 8),))
    master = normal_values(splits[2], (N_DP * CAP_OLD, 3, FF), 1.0, 6.0, ((0, 8), (2, 4)), jnp.float32)
    moment_one = normal_values(splits[3], (N_DP * CAP_OLD, 3, FF), 1.0, 6.0, ((0, 8), (2, 4)), jnp.float32)
    moment_two = jnp.clip(jnp.exp(math.log(5.0) - 4.6051702 * jax.random.uniform(splits[4], (N_DP * CAP_OLD, 3, FF), jnp.float32) ** level_of(splits[4], (N_DP * CAP_OLD, 3, FF), ((0, 8), (2, 4)), -0.2, 0.2)), 0.05, 5.0)
    old_offsets = draw_old_offsets(jax.random.fold_in(splits[7], 71), 0)
    new_offsets = draw_new_offsets(jax.random.fold_in(splits[7], 71), 0)
    return dict(tokens=tokens, out_grad=out_grad, master=master, moment_one=moment_one, moment_two=moment_two, old_offsets=old_offsets, new_offsets=new_offsets)


beta_one = 0.9
beta_two = 0.95
learn_rate = 0.01
decay_rate = 0.1
adam_eps = 1e-08
bias_one = 1.0 - 0.9 ** 10
bias_two = 1.0 - 0.95 ** 10

def lookup(small_table, wanted):
    matches = wanted[..., None] == jnp.arange(small_table.shape[0], dtype=jnp.int32)
    return lax.optimization_barrier(jnp.sum(jnp.where(matches, small_table, 0), axis=-1)).astype(jnp.int32)

def unpack(packed, offsets, capacity):
    row_index = jnp.arange(FEATURE_WIDTH, dtype=jnp.int32)
    owner_index = lax.optimization_barrier(jnp.sum((offsets[1:N_DP][None, :] <= row_index[:, None]).astype(jnp.int32), axis=1)).astype(jnp.int32)
    slot_index = owner_index * capacity + row_index - lookup(offsets, owner_index)
    return jnp.take(packed, slot_index.astype(jnp.int32), axis=0)

def pack(full_rows, offsets, capacity):
    slot_index = jnp.arange(N_DP * capacity, dtype=jnp.int32)
    owner_index = slot_index // capacity
    local_index = slot_index - owner_index * capacity
    row_start = lookup(offsets, owner_index)
    in_range = local_index < lookup(offsets, owner_index + 1) - row_start
    row_index = jnp.clip(row_start + local_index, 0, FEATURE_WIDTH - 1).astype(jnp.int32)
    picked = jnp.take(full_rows, row_index, axis=0)
    return jnp.where(in_range[:, None, None, None], picked, 0.0)

def adam_step(master_rows, first_rows, second_rows, grads):
    first_new = beta_one * first_rows + (1.0 - beta_one) * grads
    second_new = beta_two * second_rows + (1.0 - beta_two) * grads * grads
    update = first_new / bias_one / (jnp.sqrt(second_new / bias_two) + adam_eps)
    master_new = master_rows - learn_rate * (update + decay_rate * master_rows)
    return (master_new, first_new, second_new)

def reference(tokens, out_grad, master, moment_one, moment_two, old_offsets, new_offsets):
    full_rows = unpack(jnp.stack([master, moment_one, moment_two], axis=1), old_offsets, CAP_OLD)
    weights = full_rows[:, 0].astype(jnp.bfloat16)
    gate_weight = weights[:, 0]
    up_weight = weights[:, 1]
    down_weight = weights[:, 2]
    scale_in = FEATURE_WIDTH ** (-0.5)
    scale_hidden = FF ** (-0.5)
    block_width = FF // N_MP
    down_blocks = down_weight.astype(jnp.float32).reshape(FEATURE_WIDTH, N_MP, block_width)
    live_flags = new_offsets[1:] != new_offsets[:-1]

    def one_group(grad_total, inputs):
        group_tokens, group_upstream, live_flag = inputs
        upstream = jnp.where(live_flag, group_upstream, jnp.zeros_like(group_upstream))
        gate_act = jnp.dot(group_tokens, gate_weight, preferred_element_type=jnp.float32) * scale_in
        up_act = jnp.dot(group_tokens, up_weight, preferred_element_type=jnp.float32) * scale_in
        sigmoid_gate = jax.nn.sigmoid(gate_act)
        hidden = (gate_act * sigmoid_gate * up_act).astype(jnp.bfloat16)
        hidden_blocks = hidden.astype(jnp.float32).reshape(TOK_DEV, N_MP, block_width)
        partial_value = jnp.einsum('tcf,dcf->ctd', hidden_blocks, down_blocks, precision=lax.Precision.HIGHEST) * scale_hidden
        partial_value = jnp.where(live_flag, partial_value, 0.0).astype(jnp.bfloat16)
        group_output = lax.optimization_barrier(jnp.sum(lax.optimization_barrier(partial_value).astype(jnp.float32), axis=0)).astype(jnp.bfloat16)
        back_grad = jnp.dot(upstream, down_weight, preferred_element_type=jnp.float32) * scale_hidden
        gate_grad = (back_grad * up_act * sigmoid_gate * (1.0 + gate_act * (1.0 - sigmoid_gate))).astype(jnp.bfloat16)
        up_grad = (back_grad * gate_act * sigmoid_gate).astype(jnp.bfloat16)
        term_rows = jnp.stack([jnp.dot(group_tokens.T, gate_grad, preferred_element_type=jnp.float32) * scale_in, jnp.dot(group_tokens.T, up_grad, preferred_element_type=jnp.float32) * scale_in, jnp.dot(upstream.T, hidden, preferred_element_type=jnp.float32) * scale_hidden], axis=1)
        rounded = lax.optimization_barrier(term_rows.astype(jnp.bfloat16)).astype(jnp.float32)
        return (grad_total + rounded, group_output)
    grad_total, outputs = lax.scan(one_group, jnp.zeros((FEATURE_WIDTH, 3, FF), jnp.float32), (tokens.reshape(N_DP, TOK_DEV, FEATURE_WIDTH), out_grad.reshape(N_DP, TOK_DEV, FEATURE_WIDTH), live_flags))
    new_rows = jnp.stack(adam_step(full_rows[:, 0], full_rows[:, 1], full_rows[:, 2], grad_total), axis=1)
    packed = pack(new_rows, new_offsets, CAP_NEW)
    return (packed[:, 0], packed[:, 1], packed[:, 2], outputs.reshape(TOKENS, FEATURE_WIDTH))
```

```python
import functools

import jax
import jax.numpy as jnp
from jax import lax
from jax.experimental import pallas as pl
from jax.experimental.pallas import tpu as pltpu
from jax.sharding import PartitionSpec as P


FEATURE_WIDTH = 2048
FF = 7168


beta_one = 0.9
beta_two = 0.95
learn_rate = 0.01
decay_rate = 0.1
adam_eps = 1e-08
bias_one = 1.0 - 0.9**10
bias_two = 1.0 - 0.95**10


def passed_along(value, axis, by):
    peers = lax.axis_size(axis)
    pairs = [(i, i + by) for i in range(peers) if 0 <= i + by < peers]
    return lax.ppermute(value, axis, pairs)


def lookup(small_table, wanted):
    matches = wanted[..., None] == jnp.arange(small_table.shape[0], dtype=jnp.int32)
    return jnp.sum(jnp.where(matches, small_table, 0), axis=-1)


def row_layout(row_count, capacity, offsets):
    row_index = jnp.arange(row_count, dtype=jnp.int32)
    owner_index = row_index // capacity
    local_index = row_index - owner_index * capacity
    row_start = lookup(offsets, owner_index)
    in_range = local_index < lookup(offsets, owner_index + 1) - row_start
    target = jnp.clip(row_start + local_index, 0, FEATURE_WIDTH - 1)
    return (target, in_range)


def adam_step(master_rows, first_rows, second_rows, grads):
    first_new = beta_one * first_rows + (1.0 - beta_one) * grads
    second_new = beta_two * second_rows + (1.0 - beta_two) * grads * grads
    update = first_new / bias_one / (jnp.sqrt(second_new / bias_two) + adam_eps)
    master_new = master_rows - learn_rate * (update + decay_rate * master_rows)
    return (master_new, first_new, second_new)


def reshard(states, old_offsets, new_offsets, capacity_new):
    capacity_old = states.shape[0]
    from_left = passed_along(states.astype(jnp.bfloat16), "dp", 1).astype(states.dtype)
    device_index = lax.axis_index("dp")
    local_index = jnp.arange(capacity_new, dtype=jnp.int32)
    row_start = lookup(new_offsets, device_index)
    row_count = lookup(new_offsets, device_index + 1) - row_start
    in_range = local_index < row_count
    row_index = jnp.clip(row_start + local_index, 0, FEATURE_WIDTH - 1)
    owner_index = jnp.sum(
        (old_offsets[1:-1][None, :] <= row_index[:, None]).astype(jnp.int32), axis=1
    )
    slot_index = (
        (owner_index - device_index + 1) * capacity_old
        + row_index
        - lookup(old_offsets, owner_index)
    )
    neighbours = jnp.concatenate([from_left, states], axis=0)
    picked = jnp.take(neighbours, slot_index, axis=0, mode="clip")
    return jnp.where(in_range[:, None, None, None], picked, 0.0)


def train_pass(tokens, upstream, weights, layout, capacity, live_flag):
    columns = weights.shape[2]
    scale_in = FEATURE_WIDTH ** (-0.5)
    scale_hidden = FF ** (-0.5)
    contract_rows = (((0,), (0,)), ((), ()))
    shard_piece = lax.all_gather(weights, "dp", axis=0, tiled=True)
    down_rows = jnp.zeros((FEATURE_WIDTH, columns), jnp.bfloat16)
    target, in_range = row_layout(shard_piece.shape[0], capacity, layout)
    shard_piece = jnp.where(in_range[:, None, None], shard_piece, jnp.zeros_like(shard_piece))
    token_columns = jnp.take(tokens, target, axis=1, mode="clip")
    upstream_columns = jnp.take(upstream, target, axis=1, mode="clip")
    gate_sum = jnp.dot(token_columns, shard_piece[:, 0], preferred_element_type=jnp.float32)
    up_sum = jnp.dot(token_columns, shard_piece[:, 1], preferred_element_type=jnp.float32)
    back_sum = jnp.dot(upstream_columns, shard_piece[:, 2], preferred_element_type=jnp.float32)
    placed = jnp.where(in_range, target, FEATURE_WIDTH)
    down_rows = down_rows.at[placed].set(shard_piece[:, 2], mode="drop")
    gate_sum, up_sum, back_sum, down_rows = (gate_sum, up_sum, back_sum, down_rows)
    gate_act = gate_sum * scale_in
    up_act = up_sum * scale_in
    back_grad = back_sum * scale_hidden
    sigmoid_gate = jax.nn.sigmoid(gate_act)
    hidden = (gate_act * sigmoid_gate * up_act).astype(jnp.bfloat16)
    partial_value = (
        lax.dot_general(
            hidden, down_rows, (((1,), (1,)), ((), ())), preferred_element_type=jnp.float32
        )
        * scale_hidden
    )
    partial_value = jnp.where(live_flag, partial_value, 0.0)
    layer_output = lax.psum_scatter(
        partial_value.astype(jnp.bfloat16), "mp", scatter_dimension=1, tiled=True
    )
    gate_grad = (
        back_grad * up_act * sigmoid_gate * (1.0 + gate_act * (1.0 - sigmoid_gate))
    ).astype(jnp.bfloat16)
    up_grad = (back_grad * gate_act * sigmoid_gate).astype(jnp.bfloat16)
    target, in_range = row_layout(lax.axis_size("dp") * capacity, capacity, layout)
    token_columns = jnp.take(tokens, target, axis=1, mode="clip")
    upstream_columns = jnp.take(upstream, target, axis=1, mode="clip")
    gate_part = (
        lax.dot_general(token_columns, gate_grad, contract_rows, preferred_element_type=jnp.float32)
        * scale_in
    )
    up_part = (
        lax.dot_general(token_columns, up_grad, contract_rows, preferred_element_type=jnp.float32)
        * scale_in
    )
    down_part = (
        lax.dot_general(upstream_columns, hidden, contract_rows, preferred_element_type=jnp.float32)
        * scale_hidden
    )
    stacked = jnp.stack([gate_part, up_part, down_part], axis=1)
    grads = lax.psum_scatter(
        jnp.where(in_range[:, None, None], stacked, 0.0).astype(jnp.bfloat16),
        "dp",
        scatter_dimension=0,
        tiled=True,
    ).astype(jnp.float32)
    return (grads, layer_output)


def body(tokens, out_grad, master, moment_one, moment_two, old_offsets, new_offsets):
    devices = lax.axis_size("dp")
    shard_rows = FEATURE_WIDTH // devices
    jitter_rows = shard_rows // (2 * (devices - 1)) + 2
    capacity_new = shard_rows + shard_rows // 4 + 2 * jitter_rows
    device_index = lax.axis_index("dp")
    live_flag = lookup(new_offsets, device_index + 1) != lookup(new_offsets, device_index)
    upstream = jnp.where(live_flag, out_grad, jnp.zeros_like(out_grad))
    states = jnp.stack([master, moment_one, moment_two], axis=1)
    weights = states[:, 0].astype(jnp.bfloat16)
    grads, layer_output = train_pass(
        tokens, upstream, weights, old_offsets, states.shape[0], live_flag
    )
    updated = jnp.stack(adam_step(states[:, 0], states[:, 1], states[:, 2], grads), axis=1)
    updated = reshard(updated, old_offsets, new_offsets, capacity_new)
    return (updated[:, 0], updated[:, 1], updated[:, 2], layer_output)


ANY = pl.BlockSpec(memory_space=pl.ANY)
WHOLE = pl.BlockSpec(memory_space=pltpu.VMEM)


def remote(source, target, send, recv, **where):
    return pltpu.make_async_remote_copy(
        src_ref=source,
        dst_ref=target,
        send_sem=send,
        recv_sem=recv,
        device_id=where,
        device_id_type=pl.DeviceIdType.MESH,
    )


def greet(peers):
    me = lax.axis_index("dp")
    unit = lax.axis_index("mp")
    barrier = pltpu.get_barrier_semaphore()
    for off in range(1, peers):
        pl.semaphore_signal(
            barrier,
            inc=1,
            device_id={"dp": (me + off) % peers},
            device_id_type=pl.DeviceIdType.MESH,
        )
    for other in (other_core(unit), other_chip(unit)):
        pl.semaphore_signal(
            barrier, inc=1, device_id={"mp": other}, device_id_type=pl.DeviceIdType.MESH
        )
    pl.semaphore_wait(barrier, peers + 1)


IDLE = 0


def first_column(dp, width):
    return pl.multiple_of(jnp.maximum(dp - 1, 0) * width, 128)


def other_core(unit):
    return unit + 1 - 2 * (unit % 2)


def other_chip(unit):
    return (unit + 2) % 4


def spread_kernel(peers, width, weights, tokens, upstream, far, blocks, all_tokens, all_upstream,
                  crossed_far, w_send, w_recv, z_send, z_recv, y_send, y_recv, x_send, x_recv,
                  c_send, c_recv, f_send, f_recv, own_sem):
    me = lax.axis_index("dp")
    unit = lax.axis_index("mp")
    planes = peers // 2
    z, y = me // 2, me % 2
    core, chip = other_core(unit), other_chip(unit)
    kinds = weights.shape[0]
    group = tokens.shape[0]
    piece = group // 4
    sources = (tokens, upstream)
    wholes = (all_tokens, all_upstream)
    beside = z * 2 + 1 - y

    def owner(shift, same):
        return (z + shift) * 2 + (y if same else 1 - y)

    def quarter(which, dp, unit):
        return wholes[which].at[pl.ds(pl.multiple_of(dp * group + unit * piece, piece), piece)]

    def mine(which):
        return sources[which].at[pl.ds(pl.multiple_of(unit * piece, piece), piece)]

    def along_y(which):
        return remote(
            mine(which), quarter(which, me, unit), y_send.at[which], y_recv.at[which], dp=beside
        )

    def along_y_in(which):
        here = quarter(which, beside, unit)
        return remote(here, here, y_send.at[which], y_recv.at[which], dp=beside)

    def z_slot(dz, step):
        return step + (planes if dz < 0 else 0)

    def along_z(which, dz, step, same):
        there = quarter(which, owner(-dz * step, same), unit)
        slot = z_slot(dz, step)
        return remote(
            mine(which) if step == 0 and same else there, there,
            z_send.at[which, slot, same], z_recv.at[which, slot, same], dp=(z + dz) * 2 + y,
        )

    def along_z_in(which, dz, step, same):
        here = quarter(which, owner(-dz * step, same), unit)
        slot = z_slot(dz, step - 1)
        return remote(
            here, here, z_send.at[which, slot, same], z_recv.at[which, slot, same],
            dp=(z - dz) * 2 + y,
        )

    def slot_of(shift, same):
        return 2 * (shift + planes - 1) + same

    def along_x(which, shift, same):
        here = quarter(which, owner(shift, same), unit)
        slot = slot_of(shift, same)
        return remote(here, here, x_send.at[which, slot], x_recv.at[which, slot], mp=chip)

    def along_x_in(which, shift, same):
        here = quarter(which, owner(shift, same), chip)
        slot = slot_of(shift, same)
        return remote(here, here, x_send.at[which, slot], x_recv.at[which, slot], mp=chip)

    def to_core(which, shift, same, crossed):
        here = quarter(which, owner(shift, same), chip if crossed else unit)
        slot = slot_of(shift, same)
        return remote(
            here, here, c_send.at[which, slot, crossed], c_recv.at[which, slot, crossed], mp=core
        )

    def to_core_in(which, shift, same, crossed):
        here = quarter(which, owner(shift, same), other_chip(core) if crossed else core)
        slot = slot_of(shift, same)
        return remote(
            here, here, c_send.at[which, slot, crossed], c_recv.at[which, slot, crossed], mp=core
        )

    def weight(off, kind):
        peer = (me + off) % peers
        return remote(
            weights.at[kind, :, pl.ds(first_column(peer, width), width)],
            blocks.at[me, :, pl.ds(kind * width, width)],
            w_send.at[off - 1, kind], w_recv.at[off - 1, kind], dp=peer,
        )

    def weight_in(off, kind):
        peer = (me + peers - off) % peers
        here = blocks.at[peer, :, pl.ds(kind * width, width)]
        return remote(here, here, w_send.at[off - 1, kind], w_recv.at[off - 1, kind], dp=peer)

    def weights_out(offs):
        for off in offs:
            @pl.when((me + off) % peers != IDLE)
            def _():
                for kind in range(kinds):
                    weight(off, kind).start()

    def far_rows(which, kind):
        return remote(
            far.at[which, kind], crossed_far.at[which, kind],
            f_send.at[which, kind], f_recv.at[which, kind], dp=beside,
        )

    up, down = z < planes - 1, z > 0

    def each_z(act):
        for dz, further in ((1, up), (-1, down)):
            @pl.when(further)
            def _():
                act(dz)

    def each_z_in(step, act):
        for dz, further in ((1, up), (-1, down)):
            there = (z >= step) if dz > 0 else (z + step < planes)
            act(dz, there, there & further)

    greet(peers)
    for which in range(2):
        along_y(which).start()
        each_z(lambda dz: along_z(which, dz, 0, 1).start())

    own_rows = [
        pltpu.make_async_copy(
            sources[which],
            wholes[which].at[pl.ds(pl.multiple_of(me * group, group), group)],
            own_sem.at[which],
        )
        for which in range(2)
    ]
    own_rows += [
        pltpu.make_async_copy(
            weights.at[kind, :, pl.ds(first_column(me, width), width)],
            blocks.at[me, :, pl.ds(kind * width, width)],
            own_sem.at[2 + kind],
        )
        for kind in range(kinds)
    ]
    for copy in own_rows:
        copy.start()

    offsets = sorted(range(1, peers), key=lambda off: abs(2 * off - peers))
    share = -(-len(offsets) // planes)
    weights_out(offsets[:share])

    def share_on(which, shift, same):
        along_x(which, shift, same).start()
        to_core(which, shift, same, 0).start()

    for which in range(2):
        along_y_in(which).wait_recv()
        each_z(lambda dz: along_z(which, dz, 0, 0).start())
        share_on(which, 0, 0)

    for step in range(1, planes):
        for which in range(2):
            for same in (1, 0):
                def receive(dz, there, goes_on):
                    @pl.when(there)
                    def _():
                        along_z_in(which, dz, step, same).wait_recv()

                    @pl.when(goes_on)
                    def _():
                        along_z(which, dz, step, same).start()

                    @pl.when(there)
                    def _():
                        share_on(which, -dz * step, same)

                each_z_in(step, receive)
        weights_out(offsets[share * step : share * (step + 1)])
        if step == 1:
            for which in range(far.shape[0]):
                for kind in range(kinds):
                    far_rows(which, kind).start()

    def everywhere(act):
        for step in range(planes):
            for which in range(2):
                for dz in (1, -1) if step else (1,):
                    there = (z >= step) if dz > 0 else (z + step < planes)

                    @pl.when(there)
                    def _():
                        for same in (1, 0) if step else (0,):
                            act(which, -dz * step, same)

    def cross(which, shift, same):
        along_x_in(which, shift, same).wait_recv()
        to_core(which, shift, same, 1).start()

    def finish(which, shift, same):
        for crossed in range(2):
            to_core_in(which, shift, same, crossed).wait_recv()
        along_x(which, shift, same).wait_send()
        for crossed in range(2):
            to_core(which, shift, same, crossed).wait_send()

    everywhere(cross)
    everywhere(finish)

    for which in range(2):
        along_y(which).wait_send()
        for same in (1, 0):
            each_z(lambda dz: along_z(which, dz, 0, same).wait_send())
            for step in range(1, planes):
                def sent(dz, there, goes_on):
                    @pl.when(goes_on)
                    def _():
                        along_z(which, dz, step, same).wait_send()

                each_z_in(step, sent)

    for off in range(1, peers):
        @pl.when((me + off) % peers != IDLE)
        def _():
            for kind in range(kinds):
                weight(off, kind).wait_send()

    @pl.when(me != IDLE)
    def _():
        for off in range(1, peers):
            for kind in range(kinds):
                weight_in(off, kind).wait_recv()

    for which in range(far.shape[0]):
        for kind in range(kinds):
            far_rows(which, kind).wait()
    for copy in own_rows:
        copy.wait()


def spread(weights, tokens, upstream, far, peers, width):
    kinds, rows, _ = weights.shape
    group, features = tokens.shape
    planes = peers // 2
    dma = pltpu.SemaphoreType.DMA
    return pl.pallas_call(
        functools.partial(spread_kernel, peers, width),
        out_shape=(
            jax.ShapeDtypeStruct((peers, rows, kinds * width), weights.dtype),
            jax.ShapeDtypeStruct((peers * group, features), tokens.dtype),
            jax.ShapeDtypeStruct((peers * group, features), tokens.dtype),
            jax.ShapeDtypeStruct(far.shape, far.dtype),
        ),
        in_specs=[WHOLE] * 3 + [ANY],
        out_specs=[ANY] * 4,
        scratch_shapes=[
            dma((peers - 1, kinds)), dma((peers - 1, kinds)),
            dma((2, 2 * planes, 2)), dma((2, 2 * planes, 2)),
            dma((2,)), dma((2,)),
            dma((2, 4 * planes)), dma((2, 4 * planes)),
            dma((2, 4 * planes, 2)), dma((2, 4 * planes, 2)),
            dma(far.shape[:2]), dma(far.shape[:2]),
            dma((2 + kinds,)),
        ],
        compiler_params=pltpu.CompilerParams(
            collective_id=0, has_side_effects=True, vmem_limit_bytes=24 << 20
        ),
        name="spread",
    )(weights, tokens, upstream, far)


def swap_kernel(peers, width, shares, *refs):
    if shares:
        packed, parts, arrived, gathered, send, recv, own_sem, p_send, p_recv, p_own = refs
    else:
        packed, arrived, send, recv, own_sem = refs
    me = lax.axis_index("dp")
    kinds = arrived.shape[0]
    barrier = pltpu.get_barrier_semaphore()
    for off in range(1, peers):
        pl.semaphore_signal(
            barrier,
            inc=1,
            device_id={"dp": (me + off) % peers},
            device_id_type=pl.DeviceIdType.MESH,
        )
    pl.semaphore_wait(barrier, peers - 1)

    def place(dp, kind):
        return arrived.at[kind, :, pl.ds(first_column(dp, width), width)]

    def out(off, kind):
        peer = (me + off) % peers
        return remote(
            packed.at[peer, :, pl.ds(kind * width, width)], place(me, kind),
            send.at[off - 1, kind], recv.at[off - 1, kind], dp=peer,
        )

    def into(off, kind):
        peer = (me + peers - off) % peers
        here = place(peer, kind)
        return remote(here, here, send.at[off - 1, kind], recv.at[off - 1, kind], dp=peer)

    def part(off):
        peer = (me + off) % peers
        return remote(
            parts.at[peer], gathered.at[me], p_send.at[off - 1], p_recv.at[off - 1], dp=peer
        )

    def part_in(off):
        peer = (me + peers - off) % peers
        here = gathered.at[peer]
        return remote(here, here, p_send.at[off - 1], p_recv.at[off - 1], dp=peer)

    own = [
        pltpu.make_async_copy(
            packed.at[me, :, pl.ds(kind * width, width)], place(me, kind), own_sem.at[kind]
        )
        for kind in range(kinds)
    ]
    offsets = sorted(range(1, peers), key=lambda off: abs(2 * off - peers))
    if shares:
        own_part = pltpu.make_async_copy(parts.at[me], gathered.at[me], p_own)
        for off in offsets:
            part(off).start()
        own_part.start()

    @pl.when(me != IDLE)
    def _():
        for off in offsets:
            for kind in range(kinds):
                out(off, kind).start()
        for copy in own:
            copy.start()

    if shares:
        for off in offsets:
            part_in(off).wait_recv()
            part(off).wait_send()
        own_part.wait()
    for off in range(1, peers):
        @pl.when((me + peers - off) % peers != IDLE)
        def _():
            for kind in range(kinds):
                into(off, kind).wait_recv()

    @pl.when(me != IDLE)
    def _():
        for off in range(1, peers):
            for kind in range(kinds):
                out(off, kind).wait_send()
        for copy in own:
            copy.wait()


def swap(packed, kinds, columns, shares=None):
    peers, rows, across = packed.shape
    dma = pltpu.SemaphoreType.DMA
    out_shape = [jax.ShapeDtypeStruct((kinds, rows, columns), packed.dtype)]
    scratch = [dma((peers - 1, kinds)), dma((peers - 1, kinds)), dma((kinds,))]
    operands = [packed]
    if shares is not None:
        operands.append(shares)
        out_shape.append(jax.ShapeDtypeStruct(shares.shape, shares.dtype))
        scratch += [dma((peers - 1,)), dma((peers - 1,)), dma]
    return pl.pallas_call(
        functools.partial(swap_kernel, peers, across // kinds, shares is not None),
        out_shape=out_shape,
        in_specs=[WHOLE] * len(operands),
        out_specs=[ANY] * len(out_shape),
        scratch_shapes=scratch,
        compiler_params=pltpu.CompilerParams(
            collective_id=1 + len(out_shape), has_side_effects=True, vmem_limit_bytes=16 << 20
        ),
        name="swap",
    )(*operands)


STEP_ROWS = 40


def shifted(ref, which, start):
    wide = STEP_ROWS + 8
    down = start % 8
    rows = ref[which, pl.ds(pl.multiple_of(start - down, 8), wide), :]
    rows = pltpu.roll(rows.reshape(wide // 8, 8, rows.shape[1]), 8 - down, 1)
    inside = lax.broadcasted_iota(jnp.int32, rows[1:].shape, 1) < 8 - down
    return jnp.where(inside, rows[:-1], rows[1:]).reshape(STEP_ROWS, rows.shape[2])


def adam_kernel(numbers, *refs):
    owns, near, straight, relayed, grads, last_grads = refs[:3], *refs[3:8]
    outs, from_own, from_left = refs[8:11], refs[11], refs[12]
    arrived, left_skip, count, odd = numbers[0], numbers[1], numbers[2], numbers[3]
    capacity_old = owns[0].shape[1]
    capacity_new = outs[0].shape[1]
    half = near.shape[2]
    for which in range(3):
        from_own[which, pl.ds(capacity_new, capacity_old), :] = owns[which][0]
        from_left[which, pl.ds(0, half), :] = near[which, 0].astype(jnp.float32)
        far = pl.ds(half, capacity_old - half)
        value = jnp.where(odd > 0, straight[which, 0], relayed[which, 0])
        from_left[which, far, :] = value.astype(jnp.float32)
    kinds = pl.num_programs(0)
    is_last = pl.program_id(0) == kinds - 1

    def some_rows(step, carry):
        first = pl.multiple_of(step * STEP_ROWS, 8)
        slot = first + lax.broadcasted_iota(jnp.int32, (STEP_ROWS, outs[0].shape[2]), 0)
        rows = [
            jnp.where(
                slot < arrived,
                shifted(from_left, which, first + left_skip),
                shifted(from_own, which, first + capacity_new - arrived),
            )
            for which in range(3)
        ]
        here = pl.ds(first, STEP_ROWS)
        grad = jnp.where(is_last, last_grads[0, here, :], grads[0, here, :]).astype(jnp.float32)
        updated = adam_step(rows[0], rows[1], rows[2], grad)
        for which in range(3):
            outs[which][0, here, :] = jnp.where(slot < count, updated[which], 0.0)
        return carry

    lax.fori_loop(0, capacity_new // STEP_ROWS, some_rows, 0)


def adam(states, moved, grads, last_grads, numbers):
    kinds, capacity_old, columns = states[0].shape
    capacity_new = grads.shape[1]
    width = columns // 2 if columns % 256 == 0 else columns

    def block(rows):
        return pl.BlockSpec((1, rows, width), lambda kind, part, _: (kind, 0, part))

    def stacked(rows):
        return pl.BlockSpec((3, 1, rows, width), lambda kind, part, _: (0, kind, 0, part))

    first_grads = pl.BlockSpec(
        (1, capacity_new, width), lambda kind, part, _: (jnp.minimum(kind, kinds - 2), 0, part)
    )
    third_grads = pl.BlockSpec((1, capacity_new, width), lambda kind, part, _: (0, 0, part))
    return pl.pallas_call(
        adam_kernel,
        out_shape=[jax.ShapeDtypeStruct((kinds, capacity_new, columns), jnp.float32)] * 3,
        grid_spec=pltpu.PrefetchScalarGridSpec(
            num_scalar_prefetch=1,
            grid=(kinds, columns // width),
            in_specs=[block(capacity_old)] * 3
            + [stacked(value.shape[2]) for value in moved]
            + [first_grads, third_grads],
            out_specs=[block(capacity_new)] * 3,
            scratch_shapes=[
                pltpu.VMEM((3, 2 * capacity_new + 8, width), jnp.float32),
                pltpu.VMEM((3, capacity_new + capacity_old + 8, width), jnp.float32),
            ],
        ),
        compiler_params=pltpu.CompilerParams(vmem_limit_bytes=60 << 20),
        name="adam",
    )(numbers, *states, *moved, grads, last_grads)


def cast_kernel(*refs):
    owns, near, far, weights = refs[:3], refs[3], refs[4], refs[5]
    half = near.shape[2]
    for which in range(3):
        near[which, 0] = owns[which][0, :half, :].astype(near.dtype)
        far[which, 0] = owns[which][0, half:, :].astype(far.dtype)
    weights[0] = owns[0][0].astype(weights.dtype)


def cast(states):
    kinds, rows, columns = states[0].shape
    width = columns // 2 if columns % 256 == 0 else columns
    half = (rows + 15) // 16 * 8
    stacked = [(3, kinds, half, columns), (3, kinds, rows - half, columns)]
    whole = pl.BlockSpec((1, rows, width), lambda kind, part: (kind, 0, part))
    return pl.pallas_call(
        cast_kernel,
        out_shape=[jax.ShapeDtypeStruct(shape, jnp.bfloat16) for shape in stacked]
        + [jax.ShapeDtypeStruct(states[0].shape, jnp.bfloat16)],
        grid=(kinds, columns // width),
        in_specs=[whole] * 3,
        out_specs=[
            pl.BlockSpec((3, 1, shape[2], width), lambda kind, part: (0, kind, 0, part))
            for shape in stacked
        ]
        + [whole],
        compiler_params=pltpu.CompilerParams(vmem_limit_bytes=32 << 20),
        name="cast",
    )(*states)


def lane_split(columns, peers):
    return -(-columns // (peers * 128)) * 128


def product(left, right, left_dim, right_dim):
    return lax.dot_general(
        left,
        right,
        (((left_dim,), (right_dim,)), ((), ())),
        preferred_element_type=jnp.float32,
    )


def token_pass(tokens, upstream, weights, far, old_offsets, new_offsets, capacity_new):
    peers = lax.axis_size("dp")
    feature_peers = lax.axis_size("mp")
    kinds, capacity_old, columns = weights.shape
    width = lane_split(columns, peers)
    features = tokens.shape[1]
    scale_in = features ** (-0.5)
    scale_hidden = (columns * feature_peers) ** (-0.5)
    busy = lax.axis_index("dp") != IDLE

    blocks, all_tokens, all_upstream, straight = spread(
        weights, tokens, upstream, far, peers, width
    )
    blocks = blocks.reshape(peers * capacity_old, kinds * width)
    target, in_range = row_layout(peers * capacity_old, capacity_old, old_offsets)
    target = jnp.where(in_range, target, features)
    wanted = jnp.arange(features, dtype=jnp.int32)[:, None] == target[None, :]
    rows = product(wanted.astype(jnp.bfloat16), blocks, 1, 0)
    rows = jnp.where(busy, rows, 0.0).astype(jnp.bfloat16)
    rows = lax.optimization_barrier(rows)
    rows = [rows[:, kind * width : (kind + 1) * width] for kind in range(kinds)]

    gate_act = product(all_tokens, rows[0], 1, 0) * scale_in
    up_act = product(all_tokens, rows[1], 1, 0) * scale_in
    back_grad = product(all_upstream, rows[2], 1, 0) * scale_hidden
    sigmoid_gate = jax.nn.sigmoid(gate_act)
    hidden = (gate_act * sigmoid_gate * up_act).astype(jnp.bfloat16)
    gate_grad = (
        back_grad * up_act * sigmoid_gate * (1.0 + gate_act * (1.0 - sigmoid_gate))
    ).astype(jnp.bfloat16)
    up_grad = (back_grad * gate_act * sigmoid_gate).astype(jnp.bfloat16)

    partial_value = (product(hidden, rows[2], 1, 1) * scale_hidden).astype(jnp.bfloat16)
    partial_value = lax.psum_scatter(partial_value, "mp", scatter_dimension=1, tiled=True)
    shares = partial_value.reshape(peers, -1, partial_value.shape[1])

    target, in_range = row_layout(peers * capacity_new, capacity_new, new_offsets)
    target = jnp.where(in_range, target, features)
    wanted = target[:, None] == jnp.arange(features, dtype=jnp.int32)[None, :]
    wanted = wanted.astype(jnp.bfloat16)

    def packed(value):
        value = lax.optimization_barrier(value)
        value = product(wanted, value, 1, 0).astype(jnp.bfloat16)
        return value.reshape(peers, capacity_new, -1)

    grads = [
        (product(all_tokens, gate_grad, 0, 0) * scale_in).astype(jnp.bfloat16),
        (product(all_tokens, up_grad, 0, 0) * scale_in).astype(jnp.bfloat16),
    ]
    last_grads = (product(all_upstream, hidden, 0, 0) * scale_hidden).astype(jnp.bfloat16)
    first_packed = packed(jnp.concatenate(grads, axis=1))
    last_packed = packed(last_grads)
    (grads,) = swap(first_packed, kinds - 1, columns)
    last_grads, shares = swap(last_packed, 1, columns, shares)
    layer_output = jnp.sum(shares.astype(jnp.float32), axis=0).astype(jnp.bfloat16)
    return grads, last_grads, layer_output, straight


def token_body(*arguments):
    return token_step(*arguments)


def token_step(tokens, out_grad, master, moment_one, moment_two, old_offsets, new_offsets):
    devices = lax.axis_size("dp")
    capacity_old = master.shape[0]
    capacity_new = new_capacity(tokens.shape[1], devices)
    device_index = lax.axis_index("dp")
    new_start = lookup(new_offsets, device_index)
    new_end = lookup(new_offsets, device_index + 1)
    old_start = lookup(old_offsets, device_index)
    left_start = lookup(old_offsets, jnp.maximum(device_index - 1, 0))
    live_flag = new_end != new_start
    upstream = jnp.where(live_flag, out_grad, jnp.zeros_like(out_grad))

    states = [value.transpose(1, 0, 2) for value in (master, moment_one, moment_two)]
    near, far, weights = cast(states)
    near = lax.ppermute(near, "dp", [(i, i + 1) for i in range(devices - 1)])
    grads, last_grads, layer_output, straight = token_pass(
        tokens, upstream, weights, far, old_offsets, new_offsets, capacity_new
    )
    relayed = lax.ppermute(straight, "dp", [(i, i + 2) for i in range(0, devices - 2, 2)])
    moved = (near, straight, relayed)
    arrived = jnp.clip(old_start - new_start, 0, capacity_new)
    left_skip = jnp.clip(new_start - left_start, 0, capacity_old)
    numbers = jnp.stack([arrived, left_skip, new_end - new_start, device_index % 2])
    updated = adam(states, moved, grads, last_grads, numbers)
    updated = [value.transpose(1, 0, 2) for value in updated]
    layer_output = jnp.where(live_flag, layer_output, jnp.zeros_like(layer_output))
    return (updated[0], updated[1], updated[2], layer_output)


def new_capacity(features, devices):
    shard_rows = features // devices
    jitter_rows = shard_rows // (2 * (devices - 1)) + 2
    return shard_rows + shard_rows // 4 + 2 * jitter_rows


def any_body(tokens, out_grad, master, *others):
    devices = lax.axis_size("dp")
    columns = master.shape[2]
    moved_tokens = 3 * tokens.shape[0] * devices
    moved_rows = 2 * master.shape[1] * columns
    whole = (
        devices % 2 == 0
        and lax.axis_size("mp") == 4
        and tokens.shape[0] % 64 == 0
        and columns == (devices - 1) * lane_split(columns, devices)
        and new_capacity(tokens.shape[1], devices) % STEP_ROWS == 0
    )
    chosen = token_body if whole and moved_tokens <= moved_rows else body
    return chosen(tokens, out_grad, master, *others)


def solution(mesh):
    placed = (
        P("dp", None),
        P("dp", None),
        P("dp", None, "mp"),
        P("dp", None, "mp"),
        P("dp", None, "mp"),
        P(),
        P(),
    )
    return jax.shard_map(
        any_body,
        mesh=mesh,
        in_specs=placed,
        out_specs=(P("dp", None, "mp"), P("dp", None, "mp"), P("dp", None, "mp"), P("dp", "mp")),
        check_vma=False,
    )
```

```python
import functools

import jax
import jax.numpy as jnp
from jax import lax
from jax.experimental import pallas as pl
from jax.experimental.pallas import tpu as pltpu
from jax.sharding import PartitionSpec as P


FEATURE_WIDTH = 2048
FF = 7168


beta_one = 0.9
beta_two = 0.95
learn_rate = 0.01
decay_rate = 0.1
adam_eps = 1e-08
bias_one = 1.0 - 0.9**10
bias_two = 1.0 - 0.95**10


def passed_along(value, axis, by):
    peers = lax.axis_size(axis)
    pairs = [(i, i + by) for i in range(peers) if 0 <= i + by < peers]
    return lax.ppermute(value, axis, pairs)


def lookup(small_table, wanted):
    matches = wanted[..., None] == jnp.arange(small_table.shape[0], dtype=jnp.int32)
    return jnp.sum(jnp.where(matches, small_table, 0), axis=-1)


def row_layout(row_count, capacity, offsets):
    row_index = jnp.arange(row_count, dtype=jnp.int32)
    owner_index = row_index // capacity
    local_index = row_index - owner_index * capacity
    row_start = lookup(offsets, owner_index)
    in_range = local_index < lookup(offsets, owner_index + 1) - row_start
    target = jnp.clip(row_start + local_index, 0, FEATURE_WIDTH - 1)
    return (target, in_range)


def adam_step(master_rows, first_rows, second_rows, grads):
    first_new = beta_one * first_rows + (1.0 - beta_one) * grads
    second_new = beta_two * second_rows + (1.0 - beta_two) * grads * grads
    update = first_new / bias_one / (jnp.sqrt(second_new / bias_two) + adam_eps)
    master_new = master_rows - learn_rate * (update + decay_rate * master_rows)
    return (master_new, first_new, second_new)


def reshard(states, old_offsets, new_offsets, capacity_new):
    capacity_old = states.shape[0]
    from_left = passed_along(states.astype(jnp.bfloat16), "dp", 1).astype(states.dtype)
    device_index = lax.axis_index("dp")
    local_index = jnp.arange(capacity_new, dtype=jnp.int32)
    row_start = lookup(new_offsets, device_index)
    row_count = lookup(new_offsets, device_index + 1) - row_start
    in_range = local_index < row_count
    row_index = jnp.clip(row_start + local_index, 0, FEATURE_WIDTH - 1)
    owner_index = jnp.sum(
        (old_offsets[1:-1][None, :] <= row_index[:, None]).astype(jnp.int32), axis=1
    )
    slot_index = (
        (owner_index - device_index + 1) * capacity_old
        + row_index
        - lookup(old_offsets, owner_index)
    )
    neighbours = jnp.concatenate([from_left, states], axis=0)
    picked = jnp.take(neighbours, slot_index, axis=0, mode="clip")
    return jnp.where(in_range[:, None, None, None], picked, 0.0)


def train_pass(tokens, upstream, weights, layout, capacity, live_flag):
    columns = weights.shape[2]
    scale_in = FEATURE_WIDTH ** (-0.5)
    scale_hidden = FF ** (-0.5)
    contract_rows = (((0,), (0,)), ((), ()))
    shard_piece = lax.all_gather(weights, "dp", axis=0, tiled=True)
    down_rows = jnp.zeros((FEATURE_WIDTH, columns), jnp.bfloat16)
    target, in_range = row_layout(shard_piece.shape[0], capacity, layout)
    shard_piece = jnp.where(in_range[:, None, None], shard_piece, jnp.zeros_like(shard_piece))
    token_columns = jnp.take(tokens, target, axis=1, mode="clip")
    upstream_columns = jnp.take(upstream, target, axis=1, mode="clip")
    gate_sum = jnp.dot(token_columns, shard_piece[:, 0], preferred_element_type=jnp.float32)
    up_sum = jnp.dot(token_columns, shard_piece[:, 1], preferred_element_type=jnp.float32)
    back_sum = jnp.dot(upstream_columns, shard_piece[:, 2], preferred_element_type=jnp.float32)
    placed = jnp.where(in_range, target, FEATURE_WIDTH)
    down_rows = down_rows.at[placed].set(shard_piece[:, 2], mode="drop")
    gate_sum, up_sum, back_sum, down_rows = (gate_sum, up_sum, back_sum, down_rows)
    gate_act = gate_sum * scale_in
    up_act = up_sum * scale_in
    back_grad = back_sum * scale_hidden
    sigmoid_gate = jax.nn.sigmoid(gate_act)
    hidden = (gate_act * sigmoid_gate * up_act).astype(jnp.bfloat16)
    partial_value = (
        lax.dot_general(
            hidden, down_rows, (((1,), (1,)), ((), ())), preferred_element_type=jnp.float32
        )
        * scale_hidden
    )
    partial_value = jnp.where(live_flag, partial_value, 0.0)
    layer_output = lax.psum_scatter(
        partial_value.astype(jnp.bfloat16), "mp", scatter_dimension=1, tiled=True
    )
    gate_grad = (
        back_grad * up_act * sigmoid_gate * (1.0 + gate_act * (1.0 - sigmoid_gate))
    ).astype(jnp.bfloat16)
    up_grad = (back_grad * gate_act * sigmoid_gate).astype(jnp.bfloat16)
    target, in_range = row_layout(lax.axis_size("dp") * capacity, capacity, layout)
    token_columns = jnp.take(tokens, target, axis=1, mode="clip")
    upstream_columns = jnp.take(upstream, target, axis=1, mode="clip")
    gate_part = (
        lax.dot_general(token_columns, gate_grad, contract_rows, preferred_element_type=jnp.float32)
        * scale_in
    )
    up_part = (
        lax.dot_general(token_columns, up_grad, contract_rows, preferred_element_type=jnp.float32)
        * scale_in
    )
    down_part = (
        lax.dot_general(upstream_columns, hidden, contract_rows, preferred_element_type=jnp.float32)
        * scale_hidden
    )
    stacked = jnp.stack([gate_part, up_part, down_part], axis=1)
    grads = lax.psum_scatter(
        jnp.where(in_range[:, None, None], stacked, 0.0).astype(jnp.bfloat16),
        "dp",
        scatter_dimension=0,
        tiled=True,
    ).astype(jnp.float32)
    return (grads, layer_output)


def body(tokens, out_grad, master, moment_one, moment_two, old_offsets, new_offsets):
    devices = lax.axis_size("dp")
    shard_rows = FEATURE_WIDTH // devices
    jitter_rows = shard_rows // (2 * (devices - 1)) + 2
    capacity_new = shard_rows + shard_rows // 4 + 2 * jitter_rows
    device_index = lax.axis_index("dp")
    live_flag = lookup(new_offsets, device_index + 1) != lookup(new_offsets, device_index)
    upstream = jnp.where(live_flag, out_grad, jnp.zeros_like(out_grad))
    states = jnp.stack([master, moment_one, moment_two], axis=1)
    weights = states[:, 0].astype(jnp.bfloat16)
    grads, layer_output = train_pass(
        tokens, upstream, weights, old_offsets, states.shape[0], live_flag
    )
    updated = jnp.stack(adam_step(states[:, 0], states[:, 1], states[:, 2], grads), axis=1)
    updated = reshard(updated, old_offsets, new_offsets, capacity_new)
    return (updated[:, 0], updated[:, 1], updated[:, 2], layer_output)


ANY = pl.BlockSpec(memory_space=pl.ANY)
WHOLE = pl.BlockSpec(memory_space=pltpu.VMEM)


def remote(source, target, send, recv, **where):
    return pltpu.make_async_remote_copy(
        src_ref=source,
        dst_ref=target,
        send_sem=send,
        recv_sem=recv,
        device_id=where,
        device_id_type=pl.DeviceIdType.MESH,
    )


def greet(peers):
    me = lax.axis_index("dp")
    unit = lax.axis_index("mp")
    barrier = pltpu.get_barrier_semaphore()
    for off in range(1, peers):
        pl.semaphore_signal(
            barrier,
            inc=1,
            device_id={"dp": (me + off) % peers},
            device_id_type=pl.DeviceIdType.MESH,
        )
    for other in (other_core(unit), other_chip(unit)):
        pl.semaphore_signal(
            barrier, inc=1, device_id={"mp": other}, device_id_type=pl.DeviceIdType.MESH
        )
    pl.semaphore_wait(barrier, peers + 1)


IDLE = 0


def first_column(dp, width):
    return pl.multiple_of(jnp.maximum(dp - 1, 0) * width, 128)


def other_core(unit):
    return unit + 1 - 2 * (unit % 2)


def other_chip(unit):
    return (unit + 2) % 4


def spread_kernel(peers, width, weights, tokens, upstream, far, blocks, all_tokens, all_upstream,
                  crossed_far, w_send, w_recv, z_send, z_recv, y_send, y_recv, x_send, x_recv,
                  c_send, c_recv, f_send, f_recv, own_sem):
    me = lax.axis_index("dp")
    unit = lax.axis_index("mp")
    planes = peers // 2
    z, y = me // 2, me % 2
    core, chip = other_core(unit), other_chip(unit)
    kinds = weights.shape[0]
    group = tokens.shape[0]
    piece = group // 4
    sources = (tokens, upstream)
    wholes = (all_tokens, all_upstream)
    beside = z * 2 + 1 - y

    def owner(shift, same):
        return (z + shift) * 2 + (y if same else 1 - y)

    def quarter(which, dp, unit):
        return wholes[which].at[pl.ds(pl.multiple_of(dp * group + unit * piece, piece), piece)]

    def mine(which):
        return sources[which].at[pl.ds(pl.multiple_of(unit * piece, piece), piece)]

    def along_y(which):
        return remote(
            mine(which), quarter(which, me, unit), y_send.at[which], y_recv.at[which], dp=beside
        )

    def along_y_in(which):
        here = quarter(which, beside, unit)
        return remote(here, here, y_send.at[which], y_recv.at[which], dp=beside)

    def z_slot(dz, step):
        return step + (planes if dz < 0 else 0)

    def along_z(which, dz, step, same):
        there = quarter(which, owner(-dz * step, same), unit)
        slot = z_slot(dz, step)
        return remote(
            mine(which) if step == 0 and same else there, there,
            z_send.at[which, slot, same], z_recv.at[which, slot, same], dp=(z + dz) * 2 + y,
        )

    def along_z_in(which, dz, step, same):
        here = quarter(which, owner(-dz * step, same), unit)
        slot = z_slot(dz, step - 1)
        return remote(
            here, here, z_send.at[which, slot, same], z_recv.at[which, slot, same],
            dp=(z - dz) * 2 + y,
        )

    def slot_of(shift, same):
        return 2 * (shift + planes - 1) + same

    def along_x(which, shift, same):
        here = quarter(which, owner(shift, same), unit)
        slot = slot_of(shift, same)
        return remote(here, here, x_send.at[which, slot], x_recv.at[which, slot], mp=chip)

    def along_x_in(which, shift, same):
        here = quarter(which, owner(shift, same), chip)
        slot = slot_of(shift, same)
        return remote(here, here, x_send.at[which, slot], x_recv.at[which, slot], mp=chip)

    def to_core(which, shift, same, crossed):
        here = quarter(which, owner(shift, same), chip if crossed else unit)
        slot = slot_of(shift, same)
        return remote(
            here, here, c_send.at[which, slot, crossed], c_recv.at[which, slot, crossed], mp=core
        )

    def to_core_in(which, shift, same, crossed):
        here = quarter(which, owner(shift, same), other_chip(core) if crossed else core)
        slot = slot_of(shift, same)
        return remote(
            here, here, c_send.at[which, slot, crossed], c_recv.at[which, slot, crossed], mp=core
        )

    def weight(off, kind):
        peer = (me + off) % peers
        return remote(
            weights.at[kind, :, pl.ds(first_column(peer, width), width)],
            blocks.at[me, :, pl.ds(kind * width, width)],
            w_send.at[off - 1, kind], w_recv.at[off - 1, kind], dp=peer,
        )

    def weight_in(off, kind):
        peer = (me + peers - off) % peers
        here = blocks.at[peer, :, pl.ds(kind * width, width)]
        return remote(here, here, w_send.at[off - 1, kind], w_recv.at[off - 1, kind], dp=peer)

    def weights_out(offs):
        for off in offs:
            @pl.when((me + off) % peers != IDLE)
            def _():
                for kind in range(kinds):
                    weight(off, kind).start()

    def far_rows(which, kind):
        return remote(
            far.at[which, kind], crossed_far.at[which, kind],
            f_send.at[which, kind], f_recv.at[which, kind], dp=beside,
        )

    up, down = z < planes - 1, z > 0

    def each_z(act):
        for dz, further in ((1, up), (-1, down)):
            @pl.when(further)
            def _():
                act(dz)

    def each_z_in(step, act):
        for dz, further in ((1, up), (-1, down)):
            there = (z >= step) if dz > 0 else (z + step < planes)
            act(dz, there, there & further)

    greet(peers)
    for which in range(2):
        along_y(which).start()
        each_z(lambda dz: along_z(which, dz, 0, 1).start())

    own_rows = [
        pltpu.make_async_copy(
            sources[which],
            wholes[which].at[pl.ds(pl.multiple_of(me * group, group), group)],
            own_sem.at[which],
        )
        for which in range(2)
    ]
    own_rows += [
        pltpu.make_async_copy(
            weights.at[kind, :, pl.ds(first_column(me, width), width)],
            blocks.at[me, :, pl.ds(kind * width, width)],
            own_sem.at[2 + kind],
        )
        for kind in range(kinds)
    ]
    for copy in own_rows:
        copy.start()

    offsets = sorted(range(1, peers), key=lambda off: abs(2 * off - peers))
    share = -(-len(offsets) // planes)
    for which in range(far.shape[0]):
        for kind in range(kinds):
            far_rows(which, kind).start()
    weights_out(offsets[:share])

    def share_on(which, shift, same):
        along_x(which, shift, same).start()
        to_core(which, shift, same, 0).start()

    for which in range(2):
        along_y_in(which).wait_recv()
        each_z(lambda dz: along_z(which, dz, 0, 0).start())
        share_on(which, 0, 0)

    for step in range(1, planes):
        for which in range(2):
            for same in (1, 0):
                def receive(dz, there, goes_on):
                    @pl.when(there)
                    def _():
                        along_z_in(which, dz, step, same).wait_recv()

                    @pl.when(goes_on)
                    def _():
                        along_z(which, dz, step, same).start()

                    @pl.when(there)
                    def _():
                        share_on(which, -dz * step, same)

                each_z_in(step, receive)
        weights_out(offsets[share * step : share * (step + 1)])

    def everywhere(act):
        for step in range(planes):
            for which in range(2):
                for dz in (1, -1) if step else (1,):
                    there = (z >= step) if dz > 0 else (z + step < planes)

                    @pl.when(there)
                    def _():
                        for same in (1, 0) if step else (0,):
                            act(which, -dz * step, same)

    def cross(which, shift, same):
        along_x_in(which, shift, same).wait_recv()
        to_core(which, shift, same, 1).start()

    def finish(which, shift, same):
        for crossed in range(2):
            to_core_in(which, shift, same, crossed).wait_recv()
        along_x(which, shift, same).wait_send()
        for crossed in range(2):
            to_core(which, shift, same, crossed).wait_send()

    everywhere(cross)
    everywhere(finish)

    for which in range(2):
        along_y(which).wait_send()
        for same in (1, 0):
            each_z(lambda dz: along_z(which, dz, 0, same).wait_send())
            for step in range(1, planes):
                def sent(dz, there, goes_on):
                    @pl.when(goes_on)
                    def _():
                        along_z(which, dz, step, same).wait_send()

                each_z_in(step, sent)

    for off in range(1, peers):
        @pl.when((me + off) % peers != IDLE)
        def _():
            for kind in range(kinds):
                weight(off, kind).wait_send()

    @pl.when(me != IDLE)
    def _():
        for off in range(1, peers):
            for kind in range(kinds):
                weight_in(off, kind).wait_recv()

    for which in range(far.shape[0]):
        for kind in range(kinds):
            far_rows(which, kind).wait()
    for copy in own_rows:
        copy.wait()


def spread(weights, tokens, upstream, far, peers, width):
    kinds, rows, _ = weights.shape
    group, features = tokens.shape
    planes = peers // 2
    dma = pltpu.SemaphoreType.DMA
    return pl.pallas_call(
        functools.partial(spread_kernel, peers, width),
        out_shape=(
            jax.ShapeDtypeStruct((peers, rows, kinds * width), weights.dtype),
            jax.ShapeDtypeStruct((peers * group, features), tokens.dtype),
            jax.ShapeDtypeStruct((peers * group, features), tokens.dtype),
            jax.ShapeDtypeStruct(far.shape, far.dtype),
        ),
        in_specs=[WHOLE] * 3 + [ANY],
        out_specs=[ANY] * 4,
        scratch_shapes=[
            dma((peers - 1, kinds)), dma((peers - 1, kinds)),
            dma((2, 2 * planes, 2)), dma((2, 2 * planes, 2)),
            dma((2,)), dma((2,)),
            dma((2, 4 * planes)), dma((2, 4 * planes)),
            dma((2, 4 * planes, 2)), dma((2, 4 * planes, 2)),
            dma(far.shape[:2]), dma(far.shape[:2]),
            dma((2 + kinds,)),
        ],
        compiler_params=pltpu.CompilerParams(
            collective_id=0, has_side_effects=True, vmem_limit_bytes=24 << 20
        ),
        name="spread",
    )(weights, tokens, upstream, far)


def add_rows(target, left, right, step=256):
    def some(number, carry):
        here = pl.ds(pl.multiple_of(number * step, step), step)
        total = left[here, :].astype(jnp.float32) + right[here, :].astype(jnp.float32)
        target[here, :] = total.astype(target.dtype)
        return carry

    lax.fori_loop(0, target.shape[0] // step, some, 0)


class Grads:
    def __init__(self, peers, width, packed, arrived, send, recv, own_sem):
        self.peers, self.width, self.packed, self.arrived = peers, width, packed, arrived
        self.send, self.recv, self.own_sem = send, recv, own_sem
        self.me = lax.axis_index("dp")
        self.kinds = arrived.shape[0]

    def place(self, dp, kind):
        return self.arrived.at[kind, :, pl.ds(first_column(dp, self.width), self.width)]

    def rows(self, peer, kind):
        return self.packed.at[peer, :, pl.ds(kind * self.width, self.width)]

    def out(self, off, kind):
        peer = (self.me + off) % self.peers
        return remote(
            self.rows(peer, kind), self.place(self.me, kind),
            self.send.at[off - 1, kind], self.recv.at[off - 1, kind], dp=peer,
        )

    def into(self, off, kind):
        peer = (self.me + self.peers - off) % self.peers
        here = self.place(peer, kind)
        return remote(
            here, here, self.send.at[off - 1, kind], self.recv.at[off - 1, kind], dp=peer
        )

    def own(self, kind):
        return pltpu.make_async_copy(
            self.rows(self.me, kind), self.place(self.me, kind), self.own_sem.at[kind]
        )

    def start(self):
        @pl.when(self.me != IDLE)
        def _():
            for off in sorted(range(1, self.peers), key=lambda off: abs(2 * off - self.peers)):
                for kind in range(self.kinds):
                    self.out(off, kind).start()
            for kind in range(self.kinds):
                self.own(kind).start()

    def wait(self):
        for off in range(1, self.peers):
            @pl.when((self.me + self.peers - off) % self.peers != IDLE)
            def _():
                for kind in range(self.kinds):
                    self.into(off, kind).wait_recv()

        @pl.when(self.me != IDLE)
        def _():
            for off in range(1, self.peers):
                for kind in range(self.kinds):
                    self.out(off, kind).wait_send()
            for kind in range(self.kinds):
                self.own(kind).wait()


def swap_sum_kernel(peers, width, packed, partial, arrived, shares, send, recv, own_sem,
                    from_core, both_cores, from_chip, c_send, c_recv, x_send, x_recv):
    unit = lax.axis_index("mp")
    core, chip = other_core(unit), other_chip(unit)
    grads = Grads(peers, width, packed, arrived, send, recv, own_sem)
    share = partial.shape[1] // 4
    greet(peers)

    def columns(unit):
        return partial.at[:, pl.ds(pl.multiple_of(unit * share, share), share)]

    def to_core(far):
        whose = other_chip(core) if far else core
        return remote(
            columns(whose), from_core.at[far], c_send.at[far], c_recv.at[far], mp=core
        )

    across = remote(both_cores, from_chip, x_send, x_recv, mp=chip)
    for far in (1, 0):
        to_core(far).start()
    grads.start()
    to_core(1).wait_recv()
    add_rows(both_cores, columns(chip), from_core.at[1])
    to_core(0).wait_recv()
    across.start()
    add_rows(from_core.at[0], columns(unit), from_core.at[0])
    across.wait_recv()
    add_rows(shares, from_core.at[0], from_chip)
    across.wait_send()
    for far in (1, 0):
        to_core(far).wait_send()
    grads.wait()


def swap_shares_kernel(peers, width, packed, shares, arrived, gathered, send, recv, own_sem,
                       from_beside, both, y_send, y_recv, z_send, z_recv, keep_sem):
    me = lax.axis_index("dp")
    z, y = me // 2, me % 2
    planes = peers // 2
    grads = Grads(peers, width, packed, arrived, send, recv, own_sem)
    group = shares.shape[0] // peers
    barrier = pltpu.get_barrier_semaphore()
    for off in range(1, peers):
        pl.semaphore_signal(
            barrier,
            inc=1,
            device_id={"dp": (me + off) % peers},
            device_id_type=pl.DeviceIdType.MESH,
        )
    pl.semaphore_wait(barrier, peers - 1)

    def rows(dp):
        return shares.at[pl.ds(pl.multiple_of(dp * group, group), group)]

    def along_y(plane):
        return remote(
            rows(plane * 2 + 1 - y), from_beside.at[plane],
            y_send.at[plane], y_recv.at[plane], dp=z * 2 + 1 - y,
        )

    def along_z(by):
        plane = (z + by) % planes
        return remote(
            both.at[plane], gathered.at[z], z_send.at[by - 1], z_recv.at[by - 1],
            dp=plane * 2 + y,
        )

    def along_z_in(by):
        plane = (z + planes - by) % planes
        here = gathered.at[plane]
        return remote(
            here, here, z_send.at[by - 1], z_recv.at[by - 1], dp=plane * 2 + y
        )

    for plane in range(planes):
        along_y(plane).start()
    grads.start()
    for plane in range(planes):
        along_y(plane).wait_recv()
        add_rows(both.at[plane], rows(plane * 2 + y), from_beside.at[plane])
    keep = pltpu.make_async_copy(both.at[z], gathered.at[z], keep_sem)
    for plane in range(planes):
        along_y(plane).wait_send()
    for by in range(1, planes):
        along_z(by).start()
    keep.start()
    for by in range(1, planes):
        along_z_in(by).wait_recv()
        along_z(by).wait_send()
    keep.wait()
    grads.wait()


def swap(kernel, packed, columns, kinds, other, gives, more, collective_id):
    peers, rows, across = packed.shape
    dma = pltpu.SemaphoreType.DMA
    return pl.pallas_call(
        functools.partial(kernel, peers, across // kinds),
        out_shape=[
            jax.ShapeDtypeStruct((kinds, rows, columns), packed.dtype),
            jax.ShapeDtypeStruct(gives, other.dtype),
        ],
        in_specs=[WHOLE] * 2,
        out_specs=[ANY, WHOLE],
        scratch_shapes=[dma((peers - 1, kinds)), dma((peers - 1, kinds)), dma((kinds,)), *more],
        compiler_params=pltpu.CompilerParams(
            collective_id=collective_id, has_side_effects=True, vmem_limit_bytes=40 << 20
        ),
        name="swap",
    )(packed, other)


def swap_sum(packed, columns, kinds, partial):
    rows, features = partial.shape
    share = (rows, features // 4)
    dma = pltpu.SemaphoreType.DMA
    more = [
        pltpu.VMEM((2, *share), partial.dtype),
        pltpu.VMEM(share, partial.dtype),
        pltpu.VMEM(share, partial.dtype),
        dma((2,)), dma((2,)), dma, dma,
    ]
    return swap(swap_sum_kernel, packed, columns, kinds, partial, share, more, 1)


def swap_shares(packed, columns, kinds, shares):
    peers = packed.shape[0]
    planes = peers // 2
    landed = (planes, shares.shape[0] // peers, shares.shape[1])
    dma = pltpu.SemaphoreType.DMA
    more = [pltpu.VMEM(landed, shares.dtype)] * 2
    more += [dma((planes,)), dma((planes,)), dma((planes - 1,)), dma((planes - 1,)), dma]
    return swap(swap_shares_kernel, packed, columns, kinds, shares, landed, more, 2)


STEP_ROWS = 40


def shifted(ref, which, start):
    wide = STEP_ROWS + 8
    down = start % 8
    rows = ref[which, pl.ds(pl.multiple_of(start - down, 8), wide), :]
    rows = pltpu.roll(rows.reshape(wide // 8, 8, rows.shape[1]), 8 - down, 1)
    inside = lax.broadcasted_iota(jnp.int32, rows[1:].shape, 1) < 8 - down
    return jnp.where(inside, rows[:-1], rows[1:]).reshape(STEP_ROWS, rows.shape[2])


def adam_kernel(numbers, *refs):
    owns, near, straight, relayed, grads, last_grads = refs[:3], *refs[3:8]
    outs, from_own, from_left = refs[8:11], refs[11], refs[12]
    arrived, left_skip, count, odd = numbers[0], numbers[1], numbers[2], numbers[3]
    capacity_old = owns[0].shape[1]
    capacity_new = outs[0].shape[1]
    half = near.shape[2]
    for which in range(3):
        from_own[which, pl.ds(capacity_new, capacity_old), :] = owns[which][0]
        from_left[which, pl.ds(0, half), :] = near[which, 0].astype(jnp.float32)
        far = pl.ds(half, capacity_old - half)
        value = jnp.where(odd > 0, straight[which, 0], relayed[which, 0])
        from_left[which, far, :] = value.astype(jnp.float32)
    kinds = pl.num_programs(0)
    is_last = pl.program_id(0) == kinds - 1

    def some_rows(step, carry):
        first = pl.multiple_of(step * STEP_ROWS, 8)
        slot = first + lax.broadcasted_iota(jnp.int32, (STEP_ROWS, outs[0].shape[2]), 0)
        rows = [
            jnp.where(
                slot < arrived,
                shifted(from_left, which, first + left_skip),
                shifted(from_own, which, first + capacity_new - arrived),
            )
            for which in range(3)
        ]
        here = pl.ds(first, STEP_ROWS)
        grad = jnp.where(is_last, last_grads[0, here, :], grads[0, here, :]).astype(jnp.float32)
        updated = adam_step(rows[0], rows[1], rows[2], grad)
        for which in range(3):
            outs[which][0, here, :] = jnp.where(slot < count, updated[which], 0.0)
        return carry

    lax.fori_loop(0, capacity_new // STEP_ROWS, some_rows, 0)


def adam(states, moved, grads, last_grads, numbers):
    kinds, capacity_old, columns = states[0].shape
    capacity_new = grads.shape[1]
    width = columns // 2 if columns % 256 == 0 else columns

    def block(rows):
        return pl.BlockSpec((1, rows, width), lambda kind, part, _: (kind, 0, part))

    def stacked(rows):
        return pl.BlockSpec((3, 1, rows, width), lambda kind, part, _: (0, kind, 0, part))

    first_grads = pl.BlockSpec(
        (1, capacity_new, width), lambda kind, part, _: (jnp.minimum(kind, kinds - 2), 0, part)
    )
    third_grads = pl.BlockSpec((1, capacity_new, width), lambda kind, part, _: (0, 0, part))
    return pl.pallas_call(
        adam_kernel,
        out_shape=[jax.ShapeDtypeStruct((kinds, capacity_new, columns), jnp.float32)] * 3,
        grid_spec=pltpu.PrefetchScalarGridSpec(
            num_scalar_prefetch=1,
            grid=(kinds, columns // width),
            in_specs=[block(capacity_old)] * 3
            + [stacked(value.shape[2]) for value in moved]
            + [first_grads, third_grads],
            out_specs=[block(capacity_new)] * 3,
            scratch_shapes=[
                pltpu.VMEM((3, 2 * capacity_new + 8, width), jnp.float32),
                pltpu.VMEM((3, capacity_new + capacity_old + 8, width), jnp.float32),
            ],
        ),
        compiler_params=pltpu.CompilerParams(vmem_limit_bytes=60 << 20),
        name="adam",
    )(numbers, *states, *moved, grads, last_grads)


def cast_kernel(*refs):
    owns, near, far, weights = refs[:3], refs[3], refs[4], refs[5]
    half = near.shape[2]
    for which in range(3):
        near[which, 0] = owns[which][0, :half, :].astype(near.dtype)
        far[which, 0] = owns[which][0, half:, :].astype(far.dtype)
    weights[0] = owns[0][0].astype(weights.dtype)


def cast(states):
    kinds, rows, columns = states[0].shape
    width = columns // 2 if columns % 256 == 0 else columns
    half = (rows + 15) // 16 * 8
    stacked = [(3, kinds, half, columns), (3, kinds, rows - half, columns)]
    whole = pl.BlockSpec((1, rows, width), lambda kind, part: (kind, 0, part))
    return pl.pallas_call(
        cast_kernel,
        out_shape=[jax.ShapeDtypeStruct(shape, jnp.bfloat16) for shape in stacked]
        + [jax.ShapeDtypeStruct(states[0].shape, jnp.bfloat16)],
        grid=(kinds, columns // width),
        in_specs=[whole] * 3,
        out_specs=[
            pl.BlockSpec((3, 1, shape[2], width), lambda kind, part: (0, kind, 0, part))
            for shape in stacked
        ]
        + [whole],
        compiler_params=pltpu.CompilerParams(vmem_limit_bytes=32 << 20),
        name="cast",
    )(*states)


def unpack_kernel(numbers, block, *refs):
    rows, laid = refs[:-1], refs[-1]
    owner = pl.program_id(0)
    owners = pl.num_programs(0)
    busy = numbers[owners + 1]
    start = numbers[owner]
    count = (numbers[owner + 1] - start) * busy
    shift = start % 16
    slots, width = block.shape[1], rows[0].shape[1]
    window = (slots + 30) // 16 * 16

    @pl.when(owner == 0)
    def _():
        laid[...] = jnp.zeros_like(laid)

    slot = lax.broadcasted_iota(jnp.int32, block.shape[1:], 0)
    values = jnp.where(slot < count, block[0], jnp.zeros_like(block[0]))
    place = lax.broadcasted_iota(jnp.int32, (window, slots), 0) - shift
    wanted = place == lax.broadcasted_iota(jnp.int32, (window, slots), 1)
    found = jnp.dot(
        wanted.astype(jnp.bfloat16), values, preferred_element_type=jnp.float32
    ).astype(jnp.bfloat16)
    here = pl.ds(pl.multiple_of(start - shift, 16), window)
    laid[here, :] = laid[here, :] + found

    @pl.when(owner == owners - 1)
    def _():
        for kind, row in enumerate(rows):
            row[...] = laid[: row.shape[0], kind * width : (kind + 1) * width]


def unpack(blocks, offsets, busy, features, kinds):
    owners, slots, across = blocks.shape
    width = across // kinds
    whole = pl.BlockSpec((features, width), lambda owner, _: (0, 0))
    return pl.pallas_call(
        unpack_kernel,
        out_shape=[jax.ShapeDtypeStruct((features, width), blocks.dtype)] * kinds,
        grid_spec=pltpu.PrefetchScalarGridSpec(
            num_scalar_prefetch=1,
            grid=(owners,),
            in_specs=[pl.BlockSpec((1, slots, across), lambda owner, _: (owner, 0, 0))],
            out_specs=[whole] * kinds,
            scratch_shapes=[pltpu.VMEM((features + slots + 24, across), blocks.dtype)],
        ),
        compiler_params=pltpu.CompilerParams(vmem_limit_bytes=24 << 20),
        name="unpack",
    )(jnp.concatenate([offsets, busy.astype(jnp.int32)[None]]), blocks)


def pack_kernel(offsets, *refs):
    grads, packed = refs[:-1], refs[-1]
    features, width = grads[0].shape
    slots = packed.shape[1]
    window = (slots + 30) // 16 * 16
    owner = pl.program_id(0)
    start = offsets[owner]
    count = offsets[owner + 1] - start
    first = jnp.minimum(start - start % 16, features - window)
    slot = lax.broadcasted_iota(jnp.int32, (slots, window), 0)
    place = lax.broadcasted_iota(jnp.int32, (slots, window), 1)
    wanted = ((place - slot == start - first) & (slot < count)).astype(jnp.bfloat16)
    for kind, grad in enumerate(grads):
        found = jnp.dot(
            wanted,
            grad[pl.ds(pl.multiple_of(first, 16), window), :],
            preferred_element_type=jnp.float32,
        )
        packed[0, :, kind * width : (kind + 1) * width] = found.astype(packed.dtype)


def pack(grads, offsets, slots):
    features, width = grads[0].shape
    owners = offsets.shape[0] - 1
    across = len(grads) * width
    whole = pl.BlockSpec((features, width), lambda owner, _: (0, 0))
    return pl.pallas_call(
        pack_kernel,
        out_shape=jax.ShapeDtypeStruct((owners, slots, across), grads[0].dtype),
        grid_spec=pltpu.PrefetchScalarGridSpec(
            num_scalar_prefetch=1,
            grid=(owners,),
            in_specs=[whole] * len(grads),
            out_specs=pl.BlockSpec((1, slots, across), lambda owner, _: (owner, 0, 0)),
        ),
        compiler_params=pltpu.CompilerParams(vmem_limit_bytes=24 << 20),
        name="pack",
    )(offsets, *grads)


def lane_split(columns, peers):
    return -(-columns // (peers * 128)) * 128


def product(left, right, left_dim, right_dim):
    return lax.dot_general(
        left,
        right,
        (((left_dim,), (right_dim,)), ((), ())),
        preferred_element_type=jnp.float32,
    )


def token_pass(tokens, upstream, weights, far, old_offsets, new_offsets, capacity_new):
    peers = lax.axis_size("dp")
    feature_peers = lax.axis_size("mp")
    kinds, _, columns = weights.shape
    width = lane_split(columns, peers)
    features = tokens.shape[1]
    scale_in = features ** (-0.5)
    scale_hidden = (columns * feature_peers) ** (-0.5)
    busy = lax.axis_index("dp") != IDLE

    blocks, all_tokens, all_upstream, straight = spread(
        weights, tokens, upstream, far, peers, width
    )
    rows = unpack(blocks, old_offsets, busy, features, kinds)

    gate_act = product(all_tokens, rows[0], 1, 0) * scale_in
    up_act = product(all_tokens, rows[1], 1, 0) * scale_in
    back_grad = product(all_upstream, rows[2], 1, 0) * scale_hidden
    sigmoid_gate = jax.nn.sigmoid(gate_act)
    hidden = (gate_act * sigmoid_gate * up_act).astype(jnp.bfloat16)
    gate_grad = (
        back_grad * up_act * sigmoid_gate * (1.0 + gate_act * (1.0 - sigmoid_gate))
    ).astype(jnp.bfloat16)
    up_grad = (back_grad * gate_act * sigmoid_gate).astype(jnp.bfloat16)

    partial_value = (product(hidden, rows[2], 1, 1) * scale_hidden).astype(jnp.bfloat16)

    grads = [
        (product(all_tokens, gate_grad, 0, 0) * scale_in).astype(jnp.bfloat16),
        (product(all_tokens, up_grad, 0, 0) * scale_in).astype(jnp.bfloat16),
    ]
    last_grads = (product(all_upstream, hidden, 0, 0) * scale_hidden).astype(jnp.bfloat16)
    first_packed = pack(grads, new_offsets, capacity_new)
    last_packed = pack([last_grads], new_offsets, capacity_new)
    grads, shares = swap_sum(first_packed, columns, kinds - 1, partial_value)
    last_grads, shares = swap_shares(last_packed, columns, 1, shares)
    layer_output = jnp.sum(shares.astype(jnp.float32), axis=0).astype(jnp.bfloat16)
    return grads, last_grads, layer_output, straight


def token_body(*arguments):
    return token_step(*arguments)


def token_step(tokens, out_grad, master, moment_one, moment_two, old_offsets, new_offsets):
    devices = lax.axis_size("dp")
    capacity_old = master.shape[0]
    capacity_new = new_capacity(tokens.shape[1], devices)
    device_index = lax.axis_index("dp")
    new_start = lookup(new_offsets, device_index)
    new_end = lookup(new_offsets, device_index + 1)
    old_start = lookup(old_offsets, device_index)
    left_start = lookup(old_offsets, jnp.maximum(device_index - 1, 0))
    live_flag = new_end != new_start
    upstream = jnp.where(live_flag, out_grad, jnp.zeros_like(out_grad))

    states = [value.transpose(1, 0, 2) for value in (master, moment_one, moment_two)]
    near, far, weights = cast(states)
    near = lax.ppermute(near, "dp", [(i, i + 1) for i in range(devices - 1)])
    grads, last_grads, layer_output, straight = token_pass(
        tokens, upstream, weights, far, old_offsets, new_offsets, capacity_new
    )
    relayed = lax.ppermute(straight, "dp", [(i, i + 2) for i in range(0, devices - 2, 2)])
    moved = (near, straight, relayed)
    arrived = jnp.clip(old_start - new_start, 0, capacity_new)
    left_skip = jnp.clip(new_start - left_start, 0, capacity_old)
    numbers = jnp.stack([arrived, left_skip, new_end - new_start, device_index % 2])
    updated = adam(states, moved, grads, last_grads, numbers)
    updated = [value.transpose(1, 0, 2) for value in updated]
    layer_output = jnp.where(live_flag, layer_output, jnp.zeros_like(layer_output))
    return (updated[0], updated[1], updated[2], layer_output)


def new_capacity(features, devices):
    shard_rows = features // devices
    jitter_rows = shard_rows // (2 * (devices - 1)) + 2
    return shard_rows + shard_rows // 4 + 2 * jitter_rows


def any_body(tokens, out_grad, master, *others):
    devices = lax.axis_size("dp")
    columns = master.shape[2]
    moved_tokens = 3 * tokens.shape[0] * devices
    moved_rows = 2 * master.shape[1] * columns
    whole = (
        devices % 2 == 0
        and lax.axis_size("mp") == 4
        and tokens.shape[0] % 64 == 0
        and columns == (devices - 1) * lane_split(columns, devices)
        and new_capacity(tokens.shape[1], devices) % STEP_ROWS == 0
    )
    chosen = token_body if whole and moved_tokens <= moved_rows else body
    return chosen(tokens, out_grad, master, *others)


def solution(mesh):
    placed = (
        P("dp", None),
        P("dp", None),
        P("dp", None, "mp"),
        P("dp", None, "mp"),
        P("dp", None, "mp"),
        P(),
        P(),
    )
    return jax.shard_map(
        any_body,
        mesh=mesh,
        in_specs=placed,
        out_specs=(P("dp", None, "mp"), P("dp", None, "mp"), P("dp", None, "mp"), P("dp", "mp")),
        check_vma=False,
    )
```

```python
import functools

import jax
import jax.numpy as jnp
from jax import lax
from jax.experimental import pallas as pl
from jax.experimental.pallas import tpu as pltpu
from jax.sharding import PartitionSpec as P


FEATURE_WIDTH = 2048
FF = 7168


beta_one = 0.9
beta_two = 0.95
learn_rate = 0.01
decay_rate = 0.1
adam_eps = 1e-08
bias_one = 1.0 - 0.9**10
bias_two = 1.0 - 0.95**10


def passed_along(value, axis, by):
    peers = lax.axis_size(axis)
    pairs = [(i, i + by) for i in range(peers) if 0 <= i + by < peers]
    return lax.ppermute(value, axis, pairs)


def lookup(small_table, wanted):
    matches = wanted[..., None] == jnp.arange(small_table.shape[0], dtype=jnp.int32)
    return jnp.sum(jnp.where(matches, small_table, 0), axis=-1)


def row_layout(row_count, capacity, offsets):
    row_index = jnp.arange(row_count, dtype=jnp.int32)
    owner_index = row_index // capacity
    local_index = row_index - owner_index * capacity
    row_start = lookup(offsets, owner_index)
    in_range = local_index < lookup(offsets, owner_index + 1) - row_start
    target = jnp.clip(row_start + local_index, 0, FEATURE_WIDTH - 1)
    return (target, in_range)


def adam_step(master_rows, first_rows, second_rows, grads):
    first_new = beta_one * first_rows + (1.0 - beta_one) * grads
    second_new = beta_two * second_rows + (1.0 - beta_two) * grads * grads
    update = first_new / bias_one / (jnp.sqrt(second_new / bias_two) + adam_eps)
    master_new = master_rows - learn_rate * (update + decay_rate * master_rows)
    return (master_new, first_new, second_new)


def reshard(states, old_offsets, new_offsets, capacity_new):
    capacity_old = states.shape[0]
    from_left = passed_along(states.astype(jnp.bfloat16), "dp", 1).astype(states.dtype)
    device_index = lax.axis_index("dp")
    local_index = jnp.arange(capacity_new, dtype=jnp.int32)
    row_start = lookup(new_offsets, device_index)
    row_count = lookup(new_offsets, device_index + 1) - row_start
    in_range = local_index < row_count
    row_index = jnp.clip(row_start + local_index, 0, FEATURE_WIDTH - 1)
    owner_index = jnp.sum(
        (old_offsets[1:-1][None, :] <= row_index[:, None]).astype(jnp.int32), axis=1
    )
    slot_index = (
        (owner_index - device_index + 1) * capacity_old
        + row_index
        - lookup(old_offsets, owner_index)
    )
    neighbours = jnp.concatenate([from_left, states], axis=0)
    picked = jnp.take(neighbours, slot_index, axis=0, mode="clip")
    return jnp.where(in_range[:, None, None, None], picked, 0.0)


def train_pass(tokens, upstream, weights, layout, capacity, live_flag):
    columns = weights.shape[2]
    scale_in = FEATURE_WIDTH ** (-0.5)
    scale_hidden = FF ** (-0.5)
    contract_rows = (((0,), (0,)), ((), ()))
    shard_piece = lax.all_gather(weights, "dp", axis=0, tiled=True)
    down_rows = jnp.zeros((FEATURE_WIDTH, columns), jnp.bfloat16)
    target, in_range = row_layout(shard_piece.shape[0], capacity, layout)
    shard_piece = jnp.where(in_range[:, None, None], shard_piece, jnp.zeros_like(shard_piece))
    token_columns = jnp.take(tokens, target, axis=1, mode="clip")
    upstream_columns = jnp.take(upstream, target, axis=1, mode="clip")
    gate_sum = jnp.dot(token_columns, shard_piece[:, 0], preferred_element_type=jnp.float32)
    up_sum = jnp.dot(token_columns, shard_piece[:, 1], preferred_element_type=jnp.float32)
    back_sum = jnp.dot(upstream_columns, shard_piece[:, 2], preferred_element_type=jnp.float32)
    placed = jnp.where(in_range, target, FEATURE_WIDTH)
    down_rows = down_rows.at[placed].set(shard_piece[:, 2], mode="drop")
    gate_sum, up_sum, back_sum, down_rows = (gate_sum, up_sum, back_sum, down_rows)
    gate_act = gate_sum * scale_in
    up_act = up_sum * scale_in
    back_grad = back_sum * scale_hidden
    sigmoid_gate = jax.nn.sigmoid(gate_act)
    hidden = (gate_act * sigmoid_gate * up_act).astype(jnp.bfloat16)
    partial_value = (
        lax.dot_general(
            hidden, down_rows, (((1,), (1,)), ((), ())), preferred_element_type=jnp.float32
        )
        * scale_hidden
    )
    partial_value = jnp.where(live_flag, partial_value, 0.0)
    layer_output = lax.psum_scatter(
        partial_value.astype(jnp.bfloat16), "mp", scatter_dimension=1, tiled=True
    )
    gate_grad = (
        back_grad * up_act * sigmoid_gate * (1.0 + gate_act * (1.0 - sigmoid_gate))
    ).astype(jnp.bfloat16)
    up_grad = (back_grad * gate_act * sigmoid_gate).astype(jnp.bfloat16)
    target, in_range = row_layout(lax.axis_size("dp") * capacity, capacity, layout)
    token_columns = jnp.take(tokens, target, axis=1, mode="clip")
    upstream_columns = jnp.take(upstream, target, axis=1, mode="clip")
    gate_part = (
        lax.dot_general(token_columns, gate_grad, contract_rows, preferred_element_type=jnp.float32)
        * scale_in
    )
    up_part = (
        lax.dot_general(token_columns, up_grad, contract_rows, preferred_element_type=jnp.float32)
        * scale_in
    )
    down_part = (
        lax.dot_general(upstream_columns, hidden, contract_rows, preferred_element_type=jnp.float32)
        * scale_hidden
    )
    stacked = jnp.stack([gate_part, up_part, down_part], axis=1)
    grads = lax.psum_scatter(
        jnp.where(in_range[:, None, None], stacked, 0.0).astype(jnp.bfloat16),
        "dp",
        scatter_dimension=0,
        tiled=True,
    ).astype(jnp.float32)
    return (grads, layer_output)


def body(tokens, out_grad, master, moment_one, moment_two, old_offsets, new_offsets):
    devices = lax.axis_size("dp")
    shard_rows = FEATURE_WIDTH // devices
    jitter_rows = shard_rows // (2 * (devices - 1)) + 2
    capacity_new = shard_rows + shard_rows // 4 + 2 * jitter_rows
    device_index = lax.axis_index("dp")
    live_flag = lookup(new_offsets, device_index + 1) != lookup(new_offsets, device_index)
    upstream = jnp.where(live_flag, out_grad, jnp.zeros_like(out_grad))
    states = jnp.stack([master, moment_one, moment_two], axis=1)
    weights = states[:, 0].astype(jnp.bfloat16)
    grads, layer_output = train_pass(
        tokens, upstream, weights, old_offsets, states.shape[0], live_flag
    )
    updated = jnp.stack(adam_step(states[:, 0], states[:, 1], states[:, 2], grads), axis=1)
    updated = reshard(updated, old_offsets, new_offsets, capacity_new)
    return (updated[:, 0], updated[:, 1], updated[:, 2], layer_output)


ANY = pl.BlockSpec(memory_space=pl.ANY)
WHOLE = pl.BlockSpec(memory_space=pltpu.VMEM)


def remote(source, target, send, recv, **where):
    return pltpu.make_async_remote_copy(
        src_ref=source,
        dst_ref=target,
        send_sem=send,
        recv_sem=recv,
        device_id=where,
        device_id_type=pl.DeviceIdType.MESH,
    )


def greet(peers):
    me = lax.axis_index("dp")
    unit = lax.axis_index("mp")
    barrier = pltpu.get_barrier_semaphore()
    for off in range(1, peers):
        pl.semaphore_signal(
            barrier,
            inc=1,
            device_id={"dp": (me + off) % peers},
            device_id_type=pl.DeviceIdType.MESH,
        )
    for other in (other_core(unit), other_chip(unit)):
        pl.semaphore_signal(
            barrier, inc=1, device_id={"mp": other}, device_id_type=pl.DeviceIdType.MESH
        )
    pl.semaphore_wait(barrier, peers + 1)


IDLE = 0


def first_column(dp, width):
    return pl.multiple_of(jnp.maximum(dp - 1, 0) * width, 128)


def other_core(unit):
    return unit + 1 - 2 * (unit % 2)


def other_chip(unit):
    return (unit + 2) % 4


def spread_kernel(peers, width, weights, tokens, upstream, far, near, blocks, all_tokens,
                  all_upstream, crossed, crossed_rest, hopped, relayed, n_send, n_recv, w_send, w_recv, z_send, z_recv, y_send, y_recv, x_send, x_recv,
                  c_send, c_recv, f_send, f_recv, own_sem):
    me = lax.axis_index("dp")
    unit = lax.axis_index("mp")
    planes = peers // 2
    z, y = me // 2, me % 2
    core, chip = other_core(unit), other_chip(unit)
    kinds = weights.shape[0]
    group = tokens.shape[0]
    piece = group // 4
    sources = (tokens, upstream)
    wholes = (all_tokens, all_upstream)
    beside = z * 2 + 1 - y

    def owner(shift, same):
        return (z + shift) * 2 + (y if same else 1 - y)

    def quarter(which, dp, unit):
        return wholes[which].at[pl.ds(pl.multiple_of(dp * group + unit * piece, piece), piece)]

    def mine(which):
        return sources[which].at[pl.ds(pl.multiple_of(unit * piece, piece), piece)]

    def along_y(which):
        return remote(
            mine(which), quarter(which, me, unit), y_send.at[which], y_recv.at[which], dp=beside
        )

    def along_y_in(which):
        here = quarter(which, beside, unit)
        return remote(here, here, y_send.at[which], y_recv.at[which], dp=beside)

    def z_slot(dz, step):
        return step + (planes if dz < 0 else 0)

    def along_z(which, dz, step, same):
        there = quarter(which, owner(-dz * step, same), unit)
        slot = z_slot(dz, step)
        return remote(
            mine(which) if step == 0 and same else there, there,
            z_send.at[which, slot, same], z_recv.at[which, slot, same], dp=(z + dz) * 2 + y,
        )

    def along_z_in(which, dz, step, same):
        here = quarter(which, owner(-dz * step, same), unit)
        slot = z_slot(dz, step - 1)
        return remote(
            here, here, z_send.at[which, slot, same], z_recv.at[which, slot, same],
            dp=(z - dz) * 2 + y,
        )

    def slot_of(shift, same):
        return 2 * (shift + planes - 1) + same

    def along_x(which, shift, same):
        here = quarter(which, owner(shift, same), unit)
        slot = slot_of(shift, same)
        return remote(here, here, x_send.at[which, slot], x_recv.at[which, slot], mp=chip)

    def along_x_in(which, shift, same):
        here = quarter(which, owner(shift, same), chip)
        slot = slot_of(shift, same)
        return remote(here, here, x_send.at[which, slot], x_recv.at[which, slot], mp=chip)

    def to_core(which, shift, same, crossed):
        here = quarter(which, owner(shift, same), chip if crossed else unit)
        slot = slot_of(shift, same)
        return remote(
            here, here, c_send.at[which, slot, crossed], c_recv.at[which, slot, crossed], mp=core
        )

    def to_core_in(which, shift, same, crossed):
        here = quarter(which, owner(shift, same), other_chip(core) if crossed else core)
        slot = slot_of(shift, same)
        return remote(
            here, here, c_send.at[which, slot, crossed], c_recv.at[which, slot, crossed], mp=core
        )

    def weight(off, kind):
        peer = (me + off) % peers
        return remote(
            weights.at[kind, :, pl.ds(first_column(peer, width), width)],
            blocks.at[me, :, pl.ds(kind * width, width)],
            w_send.at[off - 1, kind], w_recv.at[off - 1, kind], dp=peer,
        )

    def weight_in(off, kind):
        peer = (me + peers - off) % peers
        here = blocks.at[peer, :, pl.ds(kind * width, width)]
        return remote(here, here, w_send.at[off - 1, kind], w_recv.at[off - 1, kind], dp=peer)

    def weights_out(offs):
        for off in offs:
            @pl.when((me + off) % peers != IDLE)
            def _():
                for kind in range(kinds):
                    weight(off, kind).start()

    def far_rows(which, kind):
        return remote(
            far.at[which, kind], crossed_rest.at[which - 1, kind] if which else crossed.at[kind],
            f_send.at[which, kind], f_recv.at[which, kind], dp=beside,
        )

    def hop(kind):
        return remote(
            near.at[kind], hopped.at[kind], n_send.at[kind], n_recv.at[kind], dp=(z + 1) * 2 + y
        )

    def hop_in(kind):
        here = hopped.at[kind]
        return remote(here, here, n_send.at[kind], n_recv.at[kind], dp=(z - 1) * 2 + y)

    def relay(kind):
        return remote(
            crossed.at[kind], relayed.at[kind], n_send.at[kind], n_recv.at[kind],
            dp=(z + 1) * 2 + y,
        )

    def relay_in(kind):
        here = relayed.at[kind]
        return remote(here, here, n_send.at[kind], n_recv.at[kind], dp=(z - 1) * 2 + y)

    def each_hop(act, further):
        for kind in range(kinds):
            @pl.when(further & (y > 0))
            def _():
                act[0](kind)

            @pl.when(further & (y == 0))
            def _():
                act[1](kind)

    up, down = z < planes - 1, z > 0

    def each_z(act):
        for dz, further in ((1, up), (-1, down)):
            @pl.when(further)
            def _():
                act(dz)

    def each_z_in(step, act):
        for dz, further in ((1, up), (-1, down)):
            there = (z >= step) if dz > 0 else (z + step < planes)
            act(dz, there, there & further)

    greet(peers)
    for which in range(2):
        along_y(which).start()
        each_z(lambda dz: along_z(which, dz, 0, 1).start())

    own_rows = [
        pltpu.make_async_copy(
            sources[which],
            wholes[which].at[pl.ds(pl.multiple_of(me * group, group), group)],
            own_sem.at[which],
        )
        for which in range(2)
    ]
    own_rows += [
        pltpu.make_async_copy(
            weights.at[kind, :, pl.ds(first_column(me, width), width)],
            blocks.at[me, :, pl.ds(kind * width, width)],
            own_sem.at[2 + kind],
        )
        for kind in range(kinds)
    ]
    for copy in own_rows:
        copy.start()

    offsets = sorted(range(1, peers), key=lambda off: abs(2 * off - peers))
    share = -(-len(offsets) // planes)
    for which in range(far.shape[0]):
        for kind in range(kinds):
            far_rows(which, kind).start()
    weights_out(offsets[:share])

    def share_on(which, shift, same):
        along_x(which, shift, same).start()
        to_core(which, shift, same, 0).start()

    for which in range(2):
        along_y_in(which).wait_recv()
        each_z(lambda dz: along_z(which, dz, 0, 0).start())
        share_on(which, 0, 0)

    for step in range(1, planes):
        for which in range(2):
            for same in (1, 0):
                def receive(dz, there, goes_on):
                    @pl.when(there)
                    def _():
                        along_z_in(which, dz, step, same).wait_recv()

                    @pl.when(goes_on)
                    def _():
                        along_z(which, dz, step, same).start()

                    @pl.when(there)
                    def _():
                        share_on(which, -dz * step, same)

                each_z_in(step, receive)
        weights_out(offsets[share * step : share * (step + 1)])

    for kind in range(kinds):
        far_rows(0, kind).wait_recv()
    each_hop((lambda kind: hop(kind).start(), lambda kind: relay(kind).start()), up)

    def everywhere(act):
        for step in range(planes):
            for which in range(2):
                for dz in (1, -1) if step else (1,):
                    there = (z >= step) if dz > 0 else (z + step < planes)

                    @pl.when(there)
                    def _():
                        for same in (1, 0) if step else (0,):
                            act(which, -dz * step, same)

    def cross(which, shift, same):
        along_x_in(which, shift, same).wait_recv()
        to_core(which, shift, same, 1).start()

    def finish(which, shift, same):
        for crossed in range(2):
            to_core_in(which, shift, same, crossed).wait_recv()
        along_x(which, shift, same).wait_send()
        for crossed in range(2):
            to_core(which, shift, same, crossed).wait_send()

    everywhere(cross)
    everywhere(finish)

    for which in range(2):
        along_y(which).wait_send()
        for same in (1, 0):
            each_z(lambda dz: along_z(which, dz, 0, same).wait_send())
            for step in range(1, planes):
                def sent(dz, there, goes_on):
                    @pl.when(goes_on)
                    def _():
                        along_z(which, dz, step, same).wait_send()

                each_z_in(step, sent)

    for off in range(1, peers):
        @pl.when((me + off) % peers != IDLE)
        def _():
            for kind in range(kinds):
                weight(off, kind).wait_send()

    @pl.when(me != IDLE)
    def _():
        for off in range(1, peers):
            for kind in range(kinds):
                weight_in(off, kind).wait_recv()

    each_hop((lambda kind: hop(kind).wait_send(), lambda kind: relay(kind).wait_send()), up)
    each_hop(
        (lambda kind: hop_in(kind).wait_recv(), lambda kind: relay_in(kind).wait_recv()), down
    )
    for which in range(far.shape[0]):
        for kind in range(kinds):
            far_rows(which, kind).wait_send()
            if which:
                far_rows(which, kind).wait_recv()
    for copy in own_rows:
        copy.wait()


def spread(weights, tokens, upstream, far, near, peers, width):
    kinds, rows, _ = weights.shape
    group, features = tokens.shape
    planes = peers // 2
    dma = pltpu.SemaphoreType.DMA
    return pl.pallas_call(
        functools.partial(spread_kernel, peers, width),
        out_shape=(
            jax.ShapeDtypeStruct((peers, rows, kinds * width), weights.dtype),
            jax.ShapeDtypeStruct((peers * group, features), tokens.dtype),
            jax.ShapeDtypeStruct((peers * group, features), tokens.dtype),
            jax.ShapeDtypeStruct(far.shape[1:], far.dtype),
            jax.ShapeDtypeStruct((far.shape[0] - 1, *far.shape[1:]), far.dtype),
            jax.ShapeDtypeStruct(near.shape, near.dtype),
            jax.ShapeDtypeStruct(far.shape[1:], far.dtype),
        ),
        in_specs=[WHOLE] * 3 + [ANY] * 2,
        out_specs=[ANY] * 7,
        scratch_shapes=[
            dma((kinds,)), dma((kinds,)),
            dma((peers - 1, kinds)), dma((peers - 1, kinds)),
            dma((2, 2 * planes, 2)), dma((2, 2 * planes, 2)),
            dma((2,)), dma((2,)),
            dma((2, 4 * planes)), dma((2, 4 * planes)),
            dma((2, 4 * planes, 2)), dma((2, 4 * planes, 2)),
            dma(far.shape[:2]), dma(far.shape[:2]),
            dma((2 + kinds,)),
        ],
        compiler_params=pltpu.CompilerParams(
            collective_id=0, has_side_effects=True, vmem_limit_bytes=24 << 20
        ),
        name="spread",
    )(weights, tokens, upstream, far, near)


def add_rows(target, left, right, step=256):
    def some(number, carry):
        here = pl.ds(pl.multiple_of(number * step, step), step)
        total = left[here, :].astype(jnp.float32) + right[here, :].astype(jnp.float32)
        target[here, :] = total.astype(target.dtype)
        return carry

    lax.fori_loop(0, target.shape[0] // step, some, 0)


class Grads:
    def __init__(self, peers, width, packed, arrived, send, recv, own_sem):
        self.peers, self.width, self.packed, self.arrived = peers, width, packed, arrived
        self.send, self.recv, self.own_sem = send, recv, own_sem
        self.me = lax.axis_index("dp")
        self.kinds = arrived.shape[0]

    def place(self, dp, kind):
        return self.arrived.at[kind, :, pl.ds(first_column(dp, self.width), self.width)]

    def rows(self, peer, kind):
        return self.packed.at[peer, :, pl.ds(kind * self.width, self.width)]

    def out(self, off, kind):
        peer = (self.me + off) % self.peers
        return remote(
            self.rows(peer, kind), self.place(self.me, kind),
            self.send.at[off - 1, kind], self.recv.at[off - 1, kind], dp=peer,
        )

    def into(self, off, kind):
        peer = (self.me + self.peers - off) % self.peers
        here = self.place(peer, kind)
        return remote(
            here, here, self.send.at[off - 1, kind], self.recv.at[off - 1, kind], dp=peer
        )

    def own(self, kind):
        return pltpu.make_async_copy(
            self.rows(self.me, kind), self.place(self.me, kind), self.own_sem.at[kind]
        )

    def start(self):
        @pl.when(self.me != IDLE)
        def _():
            for off in sorted(range(1, self.peers), key=lambda off: abs(2 * off - self.peers)):
                for kind in range(self.kinds):
                    self.out(off, kind).start()
            for kind in range(self.kinds):
                self.own(kind).start()

    def wait(self):
        for off in range(1, self.peers):
            @pl.when((self.me + self.peers - off) % self.peers != IDLE)
            def _():
                for kind in range(self.kinds):
                    self.into(off, kind).wait_recv()

        @pl.when(self.me != IDLE)
        def _():
            for off in range(1, self.peers):
                for kind in range(self.kinds):
                    self.out(off, kind).wait_send()
            for kind in range(self.kinds):
                self.own(kind).wait()


def swap_sum_kernel(peers, width, packed, partial, arrived, shares, send, recv, own_sem,
                    from_core, both_cores, from_chip, c_send, c_recv, x_send, x_recv):
    unit = lax.axis_index("mp")
    core, chip = other_core(unit), other_chip(unit)
    grads = Grads(peers, width, packed, arrived, send, recv, own_sem)
    share = partial.shape[1] // 4
    greet(peers)

    def columns(unit):
        return partial.at[:, pl.ds(pl.multiple_of(unit * share, share), share)]

    def to_core(far):
        whose = other_chip(core) if far else core
        return remote(
            columns(whose), from_core.at[far], c_send.at[far], c_recv.at[far], mp=core
        )

    across = remote(both_cores, from_chip, x_send, x_recv, mp=chip)
    for far in (1, 0):
        to_core(far).start()
    grads.start()
    to_core(1).wait_recv()
    add_rows(both_cores, columns(chip), from_core.at[1])
    to_core(0).wait_recv()
    across.start()
    add_rows(from_core.at[0], columns(unit), from_core.at[0])
    across.wait_recv()
    add_rows(shares, from_core.at[0], from_chip)
    across.wait_send()
    for far in (1, 0):
        to_core(far).wait_send()
    grads.wait()


def swap_shares_kernel(peers, width, packed, shares, arrived, gathered, send, recv, own_sem,
                       from_beside, both, y_send, y_recv, z_send, z_recv, keep_sem):
    me = lax.axis_index("dp")
    z, y = me // 2, me % 2
    planes = peers // 2
    grads = Grads(peers, width, packed, arrived, send, recv, own_sem)
    group = shares.shape[0] // peers
    barrier = pltpu.get_barrier_semaphore()
    for off in range(1, peers):
        pl.semaphore_signal(
            barrier,
            inc=1,
            device_id={"dp": (me + off) % peers},
            device_id_type=pl.DeviceIdType.MESH,
        )
    pl.semaphore_wait(barrier, peers - 1)

    def rows(dp):
        return shares.at[pl.ds(pl.multiple_of(dp * group, group), group)]

    def along_y(plane):
        return remote(
            rows(plane * 2 + 1 - y), from_beside.at[plane],
            y_send.at[plane], y_recv.at[plane], dp=z * 2 + 1 - y,
        )

    def along_z(by):
        plane = (z + by) % planes
        return remote(
            both.at[plane], gathered.at[z], z_send.at[by - 1], z_recv.at[by - 1],
            dp=plane * 2 + y,
        )

    def along_z_in(by):
        plane = (z + planes - by) % planes
        here = gathered.at[plane]
        return remote(
            here, here, z_send.at[by - 1], z_recv.at[by - 1], dp=plane * 2 + y
        )

    for plane in range(planes):
        along_y(plane).start()
    grads.start()
    for plane in range(planes):
        along_y(plane).wait_recv()
        add_rows(both.at[plane], rows(plane * 2 + y), from_beside.at[plane])
    keep = pltpu.make_async_copy(both.at[z], gathered.at[z], keep_sem)
    for plane in range(planes):
        along_y(plane).wait_send()
    for by in range(1, planes):
        along_z(by).start()
    keep.start()
    for by in range(1, planes):
        along_z_in(by).wait_recv()
        along_z(by).wait_send()
    keep.wait()
    grads.wait()


def swap(kernel, packed, columns, kinds, other, gives, more, collective_id):
    peers, rows, across = packed.shape
    dma = pltpu.SemaphoreType.DMA
    return pl.pallas_call(
        functools.partial(kernel, peers, across // kinds),
        out_shape=[
            jax.ShapeDtypeStruct((kinds, rows, columns), packed.dtype),
            jax.ShapeDtypeStruct(gives, other.dtype),
        ],
        in_specs=[WHOLE] * 2,
        out_specs=[ANY, WHOLE],
        scratch_shapes=[dma((peers - 1, kinds)), dma((peers - 1, kinds)), dma((kinds,)), *more],
        compiler_params=pltpu.CompilerParams(
            collective_id=collective_id, has_side_effects=True, vmem_limit_bytes=40 << 20
        ),
        name="swap",
    )(packed, other)


def swap_sum(packed, columns, kinds, partial):
    rows, features = partial.shape
    share = (rows, features // 4)
    dma = pltpu.SemaphoreType.DMA
    more = [
        pltpu.VMEM((2, *share), partial.dtype),
        pltpu.VMEM(share, partial.dtype),
        pltpu.VMEM(share, partial.dtype),
        dma((2,)), dma((2,)), dma, dma,
    ]
    return swap(swap_sum_kernel, packed, columns, kinds, partial, share, more, 1)


def swap_shares(packed, columns, kinds, shares):
    peers = packed.shape[0]
    planes = peers // 2
    landed = (planes, shares.shape[0] // peers, shares.shape[1])
    dma = pltpu.SemaphoreType.DMA
    more = [pltpu.VMEM(landed, shares.dtype)] * 2
    more += [dma((planes,)), dma((planes,)), dma((planes - 1,)), dma((planes - 1,)), dma]
    return swap(swap_shares_kernel, packed, columns, kinds, shares, landed, more, 2)


STEP_ROWS = 72
STEP_COLUMNS = 896


def shifted(ref, which, start, cols):
    wide = STEP_ROWS + 8
    down = start % 8
    rows = ref[which, pl.ds(pl.multiple_of(start - down, 8), wide), cols]
    rows = pltpu.roll(rows.reshape(wide // 8, 8, rows.shape[1]), 8 - down, 1)
    inside = lax.broadcasted_iota(jnp.int32, rows[1:].shape, 1) < 8 - down
    return jnp.where(inside, rows[:-1], rows[1:]).reshape(STEP_ROWS, rows.shape[2])


def adam_kernel(numbers, *refs):
    owns, nears, straights, relays = refs[:3], refs[3:5], refs[5:7], refs[7:9]
    grads, last_grads, outs = *refs[9:11], refs[11:14]
    from_own, from_left = refs[14:]
    arrived, left_skip, count, odd = numbers[0], numbers[1], numbers[2], numbers[3]
    capacity_old = owns[0].shape[1]
    capacity_new = outs[0].shape[1]
    half = nears[0].shape[1]

    def state(pair, which):
        return pair[1][which - 1, 0] if which else pair[0][0]

    for which in range(3):
        from_own[which, pl.ds(capacity_new, capacity_old), :] = owns[which][0]
        from_left[which, pl.ds(0, half), :] = state(nears, which).astype(jnp.float32)
        far = pl.ds(half, capacity_old - half)

        @pl.when(odd > 0)
        def _():
            from_left[which, far, :] = state(straights, which).astype(jnp.float32)

        @pl.when(odd == 0)
        def _():
            from_left[which, far, :] = state(relays, which).astype(jnp.float32)

    kinds = pl.num_programs(0)
    is_last = pl.program_id(0) == kinds - 1

    pieces = outs[0].shape[2] // STEP_COLUMNS

    def some_rows(step, carry):
        first = pl.multiple_of(step // pieces * STEP_ROWS, 8)
        here = pl.ds(first, STEP_ROWS)
        cols = pl.ds(pl.multiple_of(step % pieces * STEP_COLUMNS, 128), STEP_COLUMNS)
        slot = first + lax.broadcasted_iota(jnp.int32, (STEP_ROWS, STEP_COLUMNS), 0)

        def finish(rows):
            grad = jnp.where(is_last, last_grads[0, here, cols], grads[0, here, cols])
            updated = adam_step(rows[0], rows[1], rows[2], grad.astype(jnp.float32))
            for which in range(3):
                outs[which][0, here, cols] = jnp.where(slot < count, updated[which], 0.0)

        own = first + capacity_new - arrived

        @pl.when(first < arrived)
        def _():
            finish([
                jnp.where(
                    slot < arrived,
                    shifted(from_left, which, first + left_skip, cols),
                    shifted(from_own, which, own, cols),
                )
                for which in range(3)
            ])

        @pl.when(first >= arrived)
        def _():
            finish([shifted(from_own, which, own, cols) for which in range(3)])

        return carry

    lax.fori_loop(0, capacity_new // STEP_ROWS * pieces, some_rows, 0)


def adam(states, moved, grads, last_grads, numbers):
    kinds, capacity_old, columns = states[0].shape
    capacity_new = grads.shape[1]
    width = columns // 2 if columns % 256 == 0 else columns

    def block(rows):
        return pl.BlockSpec((1, rows, width), lambda kind, part, _: (kind, 0, part))

    def given(value, parity):
        def used(numbers):
            return 1 if parity is None else 1 - (numbers[3] - parity) * (numbers[3] - parity)

        if value.ndim == 3:
            shape = (1, value.shape[1], width)
            return pl.BlockSpec(shape, lambda kind, part, n: (kind * used(n), 0, part * used(n)))
        shape = (2, 1, value.shape[2], width)
        return pl.BlockSpec(shape, lambda kind, part, n: (0, kind * used(n), 0, part * used(n)))

    first_grads = pl.BlockSpec(
        (1, capacity_new, width), lambda kind, part, _: (jnp.minimum(kind, kinds - 2), 0, part)
    )
    third_grads = pl.BlockSpec((1, capacity_new, width), lambda kind, part, _: (0, 0, part))
    return pl.pallas_call(
        adam_kernel,
        out_shape=[jax.ShapeDtypeStruct((kinds, capacity_new, columns), jnp.float32)] * 3,
        grid_spec=pltpu.PrefetchScalarGridSpec(
            num_scalar_prefetch=1,
            grid=(kinds, columns // width),
            in_specs=[block(capacity_old)] * 3
            + [given(value, parity) for pair, parity in zip(moved, (None, 1, 0)) for value in pair]
            + [first_grads, third_grads],
            out_specs=[block(capacity_new)] * 3,
            scratch_shapes=[
                pltpu.VMEM((3, 2 * capacity_new + 8, width), jnp.float32),
                pltpu.VMEM((3, capacity_new + capacity_old + 8, width), jnp.float32),
            ],
        ),
        compiler_params=pltpu.CompilerParams(vmem_limit_bytes=60 << 20),
        name="adam",
    )(numbers, *states, *(value for pair in moved for value in pair), grads, last_grads)


def cast_kernel(*refs):
    owns, near, near_rest, far, weights = refs[:3], *refs[3:]
    half = near.shape[1]
    for which in range(3):
        target = near_rest.at[which - 1, 0] if which else near.at[0]
        target[...] = owns[which][0, :half, :].astype(near.dtype)
        far[which, 0] = owns[which][0, half:, :].astype(far.dtype)
    weights[0] = owns[0][0].astype(weights.dtype)


def cast(states):
    kinds, rows, columns = states[0].shape
    width = columns // 2 if columns % 256 == 0 else columns
    half = (rows + 15) // 16 * 8

    def one(rows):
        return pl.BlockSpec((1, rows, width), lambda kind, part: (kind, 0, part))

    def several(count, rows):
        return pl.BlockSpec((count, 1, rows, width), lambda kind, part: (0, kind, 0, part))

    shapes = [
        (kinds, half, columns),
        (2, kinds, half, columns),
        (3, kinds, rows - half, columns),
        (kinds, rows, columns),
    ]
    return pl.pallas_call(
        cast_kernel,
        out_shape=[jax.ShapeDtypeStruct(shape, jnp.bfloat16) for shape in shapes],
        grid=(kinds, columns // width),
        in_specs=[one(rows)] * 3,
        out_specs=[one(half), several(2, half), several(3, rows - half), one(rows)],
        compiler_params=pltpu.CompilerParams(vmem_limit_bytes=32 << 20),
        name="cast",
    )(*states)


def unpack_kernel(numbers, block, *refs):
    rows, laid = refs[:-1], refs[-1]
    owner = pl.program_id(0)
    owners = pl.num_programs(0)
    busy = numbers[owners + 1]
    start = numbers[owner]
    count = (numbers[owner + 1] - start) * busy
    shift = start % 16
    slots, width = block.shape[1], rows[0].shape[1]
    window = (slots + 30) // 16 * 16

    @pl.when(owner == 0)
    def _():
        laid[...] = jnp.zeros_like(laid)

    slot = lax.broadcasted_iota(jnp.int32, block.shape[1:], 0)
    values = jnp.where(slot < count, block[0], jnp.zeros_like(block[0]))
    place = lax.broadcasted_iota(jnp.int32, (window, slots), 0) - shift
    wanted = place == lax.broadcasted_iota(jnp.int32, (window, slots), 1)
    found = jnp.dot(
        wanted.astype(jnp.bfloat16), values, preferred_element_type=jnp.float32
    ).astype(jnp.bfloat16)
    here = pl.ds(pl.multiple_of(start - shift, 16), window)
    laid[here, :] = laid[here, :] + found

    @pl.when(owner == owners - 1)
    def _():
        for kind, row in enumerate(rows):
            row[...] = laid[: row.shape[0], kind * width : (kind + 1) * width]


def unpack(blocks, offsets, busy, features, kinds):
    owners, slots, across = blocks.shape
    width = across // kinds
    whole = pl.BlockSpec((features, width), lambda owner, _: (0, 0))
    return pl.pallas_call(
        unpack_kernel,
        out_shape=[jax.ShapeDtypeStruct((features, width), blocks.dtype)] * kinds,
        grid_spec=pltpu.PrefetchScalarGridSpec(
            num_scalar_prefetch=1,
            grid=(owners,),
            in_specs=[pl.BlockSpec((1, slots, across), lambda owner, _: (owner, 0, 0))],
            out_specs=[whole] * kinds,
            scratch_shapes=[pltpu.VMEM((features + slots + 24, across), blocks.dtype)],
        ),
        compiler_params=pltpu.CompilerParams(vmem_limit_bytes=24 << 20),
        name="unpack",
    )(jnp.concatenate([offsets, busy.astype(jnp.int32)[None]]), blocks)


def pack_kernel(offsets, *refs):
    grads, packed = refs[:-1], refs[-1]
    features, width = grads[0].shape
    slots = packed.shape[1]
    window = (slots + 30) // 16 * 16
    owner = pl.program_id(0)
    start = offsets[owner]
    count = offsets[owner + 1] - start
    first = jnp.minimum(start - start % 16, features - window)
    slot = lax.broadcasted_iota(jnp.int32, (slots, window), 0)
    place = lax.broadcasted_iota(jnp.int32, (slots, window), 1)
    wanted = ((place - slot == start - first) & (slot < count)).astype(jnp.bfloat16)
    for kind, grad in enumerate(grads):
        found = jnp.dot(
            wanted,
            grad[pl.ds(pl.multiple_of(first, 16), window), :],
            preferred_element_type=jnp.float32,
        )
        packed[0, :, kind * width : (kind + 1) * width] = found.astype(packed.dtype)


def pack(grads, offsets, slots):
    features, width = grads[0].shape
    owners = offsets.shape[0] - 1
    across = len(grads) * width
    whole = pl.BlockSpec((features, width), lambda owner, _: (0, 0))
    return pl.pallas_call(
        pack_kernel,
        out_shape=jax.ShapeDtypeStruct((owners, slots, across), grads[0].dtype),
        grid_spec=pltpu.PrefetchScalarGridSpec(
            num_scalar_prefetch=1,
            grid=(owners,),
            in_specs=[whole] * len(grads),
            out_specs=pl.BlockSpec((1, slots, across), lambda owner, _: (owner, 0, 0)),
        ),
        compiler_params=pltpu.CompilerParams(vmem_limit_bytes=24 << 20),
        name="pack",
    )(offsets, *grads)


def lane_split(columns, peers):
    return -(-columns // (peers * 128)) * 128


def product(left, right, left_dim, right_dim):
    return lax.dot_general(
        left,
        right,
        (((left_dim,), (right_dim,)), ((), ())),
        preferred_element_type=jnp.float32,
    )


def token_pass(tokens, upstream, weights, far, near, old_offsets, new_offsets, capacity_new):
    peers = lax.axis_size("dp")
    feature_peers = lax.axis_size("mp")
    kinds, _, columns = weights.shape
    width = lane_split(columns, peers)
    features = tokens.shape[1]
    scale_in = features ** (-0.5)
    scale_hidden = (columns * feature_peers) ** (-0.5)
    busy = lax.axis_index("dp") != IDLE

    blocks, all_tokens, all_upstream, *arrived = spread(
        weights, tokens, upstream, far, near, peers, width
    )
    rows = unpack(blocks, old_offsets, busy, features, kinds)

    gate_act = product(all_tokens, rows[0], 1, 0) * scale_in
    up_act = product(all_tokens, rows[1], 1, 0) * scale_in
    back_grad = product(all_upstream, rows[2], 1, 0) * scale_hidden
    sigmoid_gate = jax.nn.sigmoid(gate_act)
    hidden = (gate_act * sigmoid_gate * up_act).astype(jnp.bfloat16)
    gate_grad = (
        back_grad * up_act * sigmoid_gate * (1.0 + gate_act * (1.0 - sigmoid_gate))
    ).astype(jnp.bfloat16)
    up_grad = (back_grad * gate_act * sigmoid_gate).astype(jnp.bfloat16)
    gate_grad, up_grad = lax.optimization_barrier((gate_grad, up_grad))

    partial_value = (product(hidden, rows[2], 1, 1) * scale_hidden).astype(jnp.bfloat16)

    grads = [
        (product(all_tokens, gate_grad, 0, 0) * scale_in).astype(jnp.bfloat16),
        (product(all_tokens, up_grad, 0, 0) * scale_in).astype(jnp.bfloat16),
    ]
    last_grads = (product(all_upstream, hidden, 0, 0) * scale_hidden).astype(jnp.bfloat16)
    first_packed = pack(grads, new_offsets, capacity_new)
    last_packed = pack([last_grads], new_offsets, capacity_new)
    grads, shares = swap_sum(first_packed, columns, kinds - 1, partial_value)
    last_grads, shares = swap_shares(last_packed, columns, 1, shares)
    layer_output = jnp.sum(shares.astype(jnp.float32), axis=0).astype(jnp.bfloat16)
    return grads, last_grads, layer_output, arrived


def token_body(*arguments):
    return token_step(*arguments)


def token_step(tokens, out_grad, master, moment_one, moment_two, old_offsets, new_offsets):
    devices = lax.axis_size("dp")
    capacity_old = master.shape[0]
    capacity_new = new_capacity(tokens.shape[1], devices)
    device_index = lax.axis_index("dp")
    new_start = lookup(new_offsets, device_index)
    new_end = lookup(new_offsets, device_index + 1)
    old_start = lookup(old_offsets, device_index)
    left_start = lookup(old_offsets, jnp.maximum(device_index - 1, 0))
    live_flag = new_end != new_start
    upstream = jnp.where(live_flag, out_grad, jnp.zeros_like(out_grad))

    states = [value.transpose(1, 0, 2) for value in (master, moment_one, moment_two)]
    near, near_rest, far, weights = cast(states)
    near_rest = lax.ppermute(near_rest, "dp", [(i, i + 1) for i in range(devices - 1)])
    grads, last_grads, layer_output, landed = token_pass(
        tokens, upstream, weights, far, near, old_offsets, new_offsets, capacity_new
    )
    straight, straight_rest, hopped, relayed = landed
    pairs = [(i, i + 1 - 2 * (i % 2)) for i in range(devices) if i != 1]
    near = lax.ppermute(jnp.where(device_index % 2 > 0, hopped, near), "dp", pairs)
    pairs = [(i, i + 2) for i in range(0, devices - 2, 2)]
    relayed_rest = lax.ppermute(straight_rest, "dp", pairs)
    moved = ((near, near_rest), (straight, straight_rest), (relayed, relayed_rest))
    arrived = jnp.clip(old_start - new_start, 0, capacity_new)
    left_skip = jnp.clip(new_start - left_start, 0, capacity_old)
    numbers = jnp.stack([arrived, left_skip, new_end - new_start, device_index % 2])
    updated = adam(states, moved, grads, last_grads, numbers)
    updated = [value.transpose(1, 0, 2) for value in updated]
    layer_output = jnp.where(live_flag, layer_output, jnp.zeros_like(layer_output))
    return (updated[0], updated[1], updated[2], layer_output)


def new_capacity(features, devices):
    shard_rows = features // devices
    jitter_rows = shard_rows // (2 * (devices - 1)) + 2
    return shard_rows + shard_rows // 4 + 2 * jitter_rows


def any_body(tokens, out_grad, master, *others):
    devices = lax.axis_size("dp")
    columns = master.shape[2]
    moved_tokens = 3 * tokens.shape[0] * devices
    moved_rows = 2 * master.shape[1] * columns
    whole = (
        devices % 2 == 0
        and lax.axis_size("mp") == 4
        and tokens.shape[0] % 64 == 0
        and columns == (devices - 1) * lane_split(columns, devices)
        and new_capacity(tokens.shape[1], devices) % STEP_ROWS == 0
        and columns % (2 * STEP_COLUMNS) == 0
    )
    chosen = token_body if whole and moved_tokens <= moved_rows else body
    return chosen(tokens, out_grad, master, *others)


def solution(mesh):
    placed = (
        P("dp", None),
        P("dp", None),
        P("dp", None, "mp"),
        P("dp", None, "mp"),
        P("dp", None, "mp"),
        P(),
        P(),
    )
    return jax.shard_map(
        any_body,
        mesh=mesh,
        in_specs=placed,
        out_specs=(P("dp", None, "mp"), P("dp", None, "mp"), P("dp", None, "mp"), P("dp", "mp")),
        check_vma=False,
    )
```

```python
import functools

import jax
import jax.numpy as jnp
from jax import lax
from jax.experimental import pallas as pl
from jax.experimental.pallas import tpu as pltpu
from jax.sharding import PartitionSpec as P


FEATURE_WIDTH = 2048
FF = 7168


beta_one = 0.9
beta_two = 0.95
learn_rate = 0.01
decay_rate = 0.1
adam_eps = 1e-08
bias_one = 1.0 - 0.9**10
bias_two = 1.0 - 0.95**10


def passed_along(value, axis, by):
    peers = lax.axis_size(axis)
    pairs = [(i, i + by) for i in range(peers) if 0 <= i + by < peers]
    return lax.ppermute(value, axis, pairs)


def lookup(small_table, wanted):
    matches = wanted[..., None] == jnp.arange(small_table.shape[0], dtype=jnp.int32)
    return jnp.sum(jnp.where(matches, small_table, 0), axis=-1)


def row_layout(row_count, capacity, offsets):
    row_index = jnp.arange(row_count, dtype=jnp.int32)
    owner_index = row_index // capacity
    local_index = row_index - owner_index * capacity
    row_start = lookup(offsets, owner_index)
    in_range = local_index < lookup(offsets, owner_index + 1) - row_start
    target = jnp.clip(row_start + local_index, 0, FEATURE_WIDTH - 1)
    return (target, in_range)


def adam_step(master_rows, first_rows, second_rows, grads):
    first_new = beta_one * first_rows + (1.0 - beta_one) * grads
    second_new = beta_two * second_rows + (1.0 - beta_two) * grads * grads
    update = first_new / bias_one / (jnp.sqrt(second_new / bias_two) + adam_eps)
    master_new = master_rows - learn_rate * (update + decay_rate * master_rows)
    return (master_new, first_new, second_new)


def reshard(states, old_offsets, new_offsets, capacity_new):
    capacity_old = states.shape[0]
    from_left = passed_along(states.astype(jnp.bfloat16), "dp", 1).astype(states.dtype)
    device_index = lax.axis_index("dp")
    local_index = jnp.arange(capacity_new, dtype=jnp.int32)
    row_start = lookup(new_offsets, device_index)
    row_count = lookup(new_offsets, device_index + 1) - row_start
    in_range = local_index < row_count
    row_index = jnp.clip(row_start + local_index, 0, FEATURE_WIDTH - 1)
    owner_index = jnp.sum(
        (old_offsets[1:-1][None, :] <= row_index[:, None]).astype(jnp.int32), axis=1
    )
    slot_index = (
        (owner_index - device_index + 1) * capacity_old
        + row_index
        - lookup(old_offsets, owner_index)
    )
    neighbours = jnp.concatenate([from_left, states], axis=0)
    picked = jnp.take(neighbours, slot_index, axis=0, mode="clip")
    return jnp.where(in_range[:, None, None, None], picked, 0.0)


def train_pass(tokens, upstream, weights, layout, capacity, live_flag):
    columns = weights.shape[2]
    scale_in = FEATURE_WIDTH ** (-0.5)
    scale_hidden = FF ** (-0.5)
    contract_rows = (((0,), (0,)), ((), ()))
    shard_piece = lax.all_gather(weights, "dp", axis=0, tiled=True)
    down_rows = jnp.zeros((FEATURE_WIDTH, columns), jnp.bfloat16)
    target, in_range = row_layout(shard_piece.shape[0], capacity, layout)
    shard_piece = jnp.where(in_range[:, None, None], shard_piece, jnp.zeros_like(shard_piece))
    token_columns = jnp.take(tokens, target, axis=1, mode="clip")
    upstream_columns = jnp.take(upstream, target, axis=1, mode="clip")
    gate_sum = jnp.dot(token_columns, shard_piece[:, 0], preferred_element_type=jnp.float32)
    up_sum = jnp.dot(token_columns, shard_piece[:, 1], preferred_element_type=jnp.float32)
    back_sum = jnp.dot(upstream_columns, shard_piece[:, 2], preferred_element_type=jnp.float32)
    placed = jnp.where(in_range, target, FEATURE_WIDTH)
    down_rows = down_rows.at[placed].set(shard_piece[:, 2], mode="drop")
    gate_sum, up_sum, back_sum, down_rows = (gate_sum, up_sum, back_sum, down_rows)
    gate_act = gate_sum * scale_in
    up_act = up_sum * scale_in
    back_grad = back_sum * scale_hidden
    sigmoid_gate = jax.nn.sigmoid(gate_act)
    hidden = (gate_act * sigmoid_gate * up_act).astype(jnp.bfloat16)
    partial_value = (
        lax.dot_general(
            hidden, down_rows, (((1,), (1,)), ((), ())), preferred_element_type=jnp.float32
        )
        * scale_hidden
    )
    partial_value = jnp.where(live_flag, partial_value, 0.0)
    layer_output = lax.psum_scatter(
        partial_value.astype(jnp.bfloat16), "mp", scatter_dimension=1, tiled=True
    )
    gate_grad = (
        back_grad * up_act * sigmoid_gate * (1.0 + gate_act * (1.0 - sigmoid_gate))
    ).astype(jnp.bfloat16)
    up_grad = (back_grad * gate_act * sigmoid_gate).astype(jnp.bfloat16)
    target, in_range = row_layout(lax.axis_size("dp") * capacity, capacity, layout)
    token_columns = jnp.take(tokens, target, axis=1, mode="clip")
    upstream_columns = jnp.take(upstream, target, axis=1, mode="clip")
    gate_part = (
        lax.dot_general(token_columns, gate_grad, contract_rows, preferred_element_type=jnp.float32)
        * scale_in
    )
    up_part = (
        lax.dot_general(token_columns, up_grad, contract_rows, preferred_element_type=jnp.float32)
        * scale_in
    )
    down_part = (
        lax.dot_general(upstream_columns, hidden, contract_rows, preferred_element_type=jnp.float32)
        * scale_hidden
    )
    stacked = jnp.stack([gate_part, up_part, down_part], axis=1)
    grads = lax.psum_scatter(
        jnp.where(in_range[:, None, None], stacked, 0.0).astype(jnp.bfloat16),
        "dp",
        scatter_dimension=0,
        tiled=True,
    ).astype(jnp.float32)
    return (grads, layer_output)


def body(tokens, out_grad, master, moment_one, moment_two, old_offsets, new_offsets):
    devices = lax.axis_size("dp")
    shard_rows = FEATURE_WIDTH // devices
    jitter_rows = shard_rows // (2 * (devices - 1)) + 2
    capacity_new = shard_rows + shard_rows // 4 + 2 * jitter_rows
    device_index = lax.axis_index("dp")
    live_flag = lookup(new_offsets, device_index + 1) != lookup(new_offsets, device_index)
    upstream = jnp.where(live_flag, out_grad, jnp.zeros_like(out_grad))
    states = jnp.stack([master, moment_one, moment_two], axis=1)
    weights = states[:, 0].astype(jnp.bfloat16)
    grads, layer_output = train_pass(
        tokens, upstream, weights, old_offsets, states.shape[0], live_flag
    )
    updated = jnp.stack(adam_step(states[:, 0], states[:, 1], states[:, 2], grads), axis=1)
    updated = reshard(updated, old_offsets, new_offsets, capacity_new)
    return (updated[:, 0], updated[:, 1], updated[:, 2], layer_output)


ANY = pl.BlockSpec(memory_space=pl.ANY)
WHOLE = pl.BlockSpec(memory_space=pltpu.VMEM)


def remote(source, target, send, recv, **where):
    return pltpu.make_async_remote_copy(
        src_ref=source,
        dst_ref=target,
        send_sem=send,
        recv_sem=recv,
        device_id=where,
        device_id_type=pl.DeviceIdType.MESH,
    )


def greet(peers):
    me = lax.axis_index("dp")
    unit = lax.axis_index("mp")
    barrier = pltpu.get_barrier_semaphore()
    for off in range(1, peers):
        pl.semaphore_signal(
            barrier,
            inc=1,
            device_id={"dp": (me + off) % peers},
            device_id_type=pl.DeviceIdType.MESH,
        )
    for other in (other_core(unit), other_chip(unit)):
        pl.semaphore_signal(
            barrier, inc=1, device_id={"mp": other}, device_id_type=pl.DeviceIdType.MESH
        )
    pl.semaphore_wait(barrier, peers + 1)


IDLE = 0


def first_column(dp, width):
    return pl.multiple_of(jnp.maximum(dp - 1, 0) * width, 128)


def other_core(unit):
    return unit + 1 - 2 * (unit % 2)


def other_chip(unit):
    return (unit + 2) % 4


def spread_kernel(peers, width, weights, tokens, upstream, far, near, first, second, blocks,
                  all_tokens, all_upstream, crossed, crossed_rest, hopped, relayed, near_rest,
                  far_rest, n_send, n_recv, w_send, w_recv, z_send, z_recv, y_send, y_recv, x_send, x_recv,
                  c_send, c_recv, f_send, f_recv, own_sem):
    me = lax.axis_index("dp")
    unit = lax.axis_index("mp")
    planes = peers // 2
    z, y = me // 2, me % 2
    core, chip = other_core(unit), other_chip(unit)
    kinds = weights.shape[0]
    group = tokens.shape[0]
    piece = group // 4
    sources = (tokens, upstream)
    wholes = (all_tokens, all_upstream)
    beside = z * 2 + 1 - y

    def owner(shift, same):
        return (z + shift) * 2 + (y if same else 1 - y)

    def quarter(which, dp, unit):
        return wholes[which].at[pl.ds(pl.multiple_of(dp * group + unit * piece, piece), piece)]

    def mine(which):
        return sources[which].at[pl.ds(pl.multiple_of(unit * piece, piece), piece)]

    def along_y(which):
        return remote(
            mine(which), quarter(which, me, unit), y_send.at[which], y_recv.at[which], dp=beside
        )

    def along_y_in(which):
        here = quarter(which, beside, unit)
        return remote(here, here, y_send.at[which], y_recv.at[which], dp=beside)

    def z_slot(dz, step):
        return step + (planes if dz < 0 else 0)

    def along_z(which, dz, step, same):
        there = quarter(which, owner(-dz * step, same), unit)
        slot = z_slot(dz, step)
        return remote(
            mine(which) if step == 0 and same else there, there,
            z_send.at[which, slot, same], z_recv.at[which, slot, same], dp=(z + dz) * 2 + y,
        )

    def along_z_in(which, dz, step, same):
        here = quarter(which, owner(-dz * step, same), unit)
        slot = z_slot(dz, step - 1)
        return remote(
            here, here, z_send.at[which, slot, same], z_recv.at[which, slot, same],
            dp=(z - dz) * 2 + y,
        )

    def slot_of(shift, same):
        return 2 * (shift + planes - 1) + same

    def along_x(which, shift, same):
        here = quarter(which, owner(shift, same), unit)
        slot = slot_of(shift, same)
        return remote(here, here, x_send.at[which, slot], x_recv.at[which, slot], mp=chip)

    def along_x_in(which, shift, same):
        here = quarter(which, owner(shift, same), chip)
        slot = slot_of(shift, same)
        return remote(here, here, x_send.at[which, slot], x_recv.at[which, slot], mp=chip)

    def to_core(which, shift, same, crossed):
        here = quarter(which, owner(shift, same), chip if crossed else unit)
        slot = slot_of(shift, same)
        return remote(
            here, here, c_send.at[which, slot, crossed], c_recv.at[which, slot, crossed], mp=core
        )

    def to_core_in(which, shift, same, crossed):
        here = quarter(which, owner(shift, same), other_chip(core) if crossed else core)
        slot = slot_of(shift, same)
        return remote(
            here, here, c_send.at[which, slot, crossed], c_recv.at[which, slot, crossed], mp=core
        )

    def weight(off, kind):
        peer = (me + off) % peers
        return remote(
            weights.at[kind, :, pl.ds(first_column(peer, width), width)],
            blocks.at[me, :, pl.ds(kind * width, width)],
            w_send.at[off - 1, kind], w_recv.at[off - 1, kind], dp=peer,
        )

    def weight_in(off, kind):
        peer = (me + peers - off) % peers
        here = blocks.at[peer, :, pl.ds(kind * width, width)]
        return remote(here, here, w_send.at[off - 1, kind], w_recv.at[off - 1, kind], dp=peer)

    def weights_out(offs):
        for off in offs:
            @pl.when((me + off) % peers != IDLE)
            def _():
                for kind in range(kinds):
                    weight(off, kind).start()

    def far_rows(which, kind):
        return remote(
            far_rest.at[which - 1, kind] if which else far.at[kind],
            crossed_rest.at[which - 1, kind] if which else crossed.at[kind],
            f_send.at[which, kind], f_recv.at[which, kind], dp=beside,
        )

    def hop(kind):
        return remote(
            near.at[kind], hopped.at[kind], n_send.at[kind], n_recv.at[kind], dp=(z + 1) * 2 + y
        )

    def hop_in(kind):
        here = hopped.at[kind]
        return remote(here, here, n_send.at[kind], n_recv.at[kind], dp=(z - 1) * 2 + y)

    def relay(kind):
        return remote(
            crossed.at[kind], relayed.at[kind], n_send.at[kind], n_recv.at[kind],
            dp=(z + 1) * 2 + y,
        )

    def relay_in(kind):
        here = relayed.at[kind]
        return remote(here, here, n_send.at[kind], n_recv.at[kind], dp=(z - 1) * 2 + y)

    def each_hop(act, further):
        for kind in range(kinds):
            @pl.when(further & (y > 0))
            def _():
                act[0](kind)

            @pl.when(further & (y == 0))
            def _():
                act[1](kind)

    up, down = z < planes - 1, z > 0

    def each_z(act):
        for dz, further in ((1, up), (-1, down)):
            @pl.when(further)
            def _():
                act(dz)

    def each_z_in(step, act):
        for dz, further in ((1, up), (-1, down)):
            there = (z >= step) if dz > 0 else (z + step < planes)
            act(dz, there, there & further)

    greet(peers)
    for which in range(2):
        along_y(which).start()
        each_z(lambda dz: along_z(which, dz, 0, 1).start())

    own_rows = [
        pltpu.make_async_copy(
            sources[which],
            wholes[which].at[pl.ds(pl.multiple_of(me * group, group), group)],
            own_sem.at[which],
        )
        for which in range(2)
    ]
    own_rows += [
        pltpu.make_async_copy(
            weights.at[kind, :, pl.ds(first_column(me, width), width)],
            blocks.at[me, :, pl.ds(kind * width, width)],
            own_sem.at[2 + kind],
        )
        for kind in range(kinds)
    ]
    for copy in own_rows:
        copy.start()

    offsets = sorted(range(1, peers), key=lambda off: abs(2 * off - peers))
    share = -(-len(offsets) // planes)
    for kind in range(kinds):
        far_rows(0, kind).start()
    weights_out(offsets[:share])

    half, rest = near_rest.shape[2], far_rest.shape[2]
    across = first.shape[2] // 2

    def halves(*refs):
        for which in range(2):
            refs[2][which, 0] = refs[which][0, :half, :].astype(near_rest.dtype)
            refs[3][which, 0] = refs[which][0, half:, :].astype(far_rest.dtype)

    pltpu.emit_pipeline(
        halves,
        grid=(kinds, 2),
        in_specs=[pl.BlockSpec((1, half + rest, across), lambda kind, part: (kind, 0, part))] * 2,
        out_specs=[
            pl.BlockSpec((2, 1, count, across), lambda kind, part: (0, kind, 0, part))
            for count in (half, rest)
        ],
    )(first, second, near_rest, far_rest)
    for which in range(1, 3):
        for kind in range(kinds):
            far_rows(which, kind).start()

    def share_on(which, shift, same):
        along_x(which, shift, same).start()
        to_core(which, shift, same, 0).start()

    for which in range(2):
        along_y_in(which).wait_recv()
        each_z(lambda dz: along_z(which, dz, 0, 0).start())
        share_on(which, 0, 0)

    for step in range(1, planes):
        for which in range(2):
            for same in (1, 0):
                def receive(dz, there, goes_on):
                    @pl.when(there)
                    def _():
                        along_z_in(which, dz, step, same).wait_recv()

                    @pl.when(goes_on)
                    def _():
                        along_z(which, dz, step, same).start()

                    @pl.when(there)
                    def _():
                        share_on(which, -dz * step, same)

                each_z_in(step, receive)
        weights_out(offsets[share * step : share * (step + 1)])

    for kind in range(kinds):
        far_rows(0, kind).wait_recv()
    each_hop((lambda kind: hop(kind).start(), lambda kind: relay(kind).start()), up)

    def everywhere(act):
        for step in range(planes):
            for which in range(2):
                for dz in (1, -1) if step else (1,):
                    there = (z >= step) if dz > 0 else (z + step < planes)

                    @pl.when(there)
                    def _():
                        for same in (1, 0) if step else (0,):
                            act(which, -dz * step, same)

    def cross(which, shift, same):
        along_x_in(which, shift, same).wait_recv()
        to_core(which, shift, same, 1).start()

    def finish(which, shift, same):
        for crossed in range(2):
            to_core_in(which, shift, same, crossed).wait_recv()
        along_x(which, shift, same).wait_send()
        for crossed in range(2):
            to_core(which, shift, same, crossed).wait_send()

    everywhere(cross)
    everywhere(finish)

    for which in range(2):
        along_y(which).wait_send()
        for same in (1, 0):
            each_z(lambda dz: along_z(which, dz, 0, same).wait_send())
            for step in range(1, planes):
                def sent(dz, there, goes_on):
                    @pl.when(goes_on)
                    def _():
                        along_z(which, dz, step, same).wait_send()

                each_z_in(step, sent)

    for off in range(1, peers):
        @pl.when((me + off) % peers != IDLE)
        def _():
            for kind in range(kinds):
                weight(off, kind).wait_send()

    @pl.when(me != IDLE)
    def _():
        for off in range(1, peers):
            for kind in range(kinds):
                weight_in(off, kind).wait_recv()

    each_hop((lambda kind: hop(kind).wait_send(), lambda kind: relay(kind).wait_send()), up)
    each_hop(
        (lambda kind: hop_in(kind).wait_recv(), lambda kind: relay_in(kind).wait_recv()), down
    )
    for which in range(3):
        for kind in range(kinds):
            far_rows(which, kind).wait_send()
            if which:
                far_rows(which, kind).wait_recv()
    for copy in own_rows:
        copy.wait()


def spread(weights, tokens, upstream, far, near, others, peers, width):
    kinds, rows, _ = weights.shape
    group, features = tokens.shape
    planes = peers // 2
    dma = pltpu.SemaphoreType.DMA
    return pl.pallas_call(
        functools.partial(spread_kernel, peers, width),
        out_shape=(
            jax.ShapeDtypeStruct((peers, rows, kinds * width), weights.dtype),
            jax.ShapeDtypeStruct((peers * group, features), tokens.dtype),
            jax.ShapeDtypeStruct((peers * group, features), tokens.dtype),
            jax.ShapeDtypeStruct(far.shape, far.dtype),
            jax.ShapeDtypeStruct((2, *far.shape), far.dtype),
            jax.ShapeDtypeStruct(near.shape, near.dtype),
            jax.ShapeDtypeStruct(far.shape, far.dtype),
            jax.ShapeDtypeStruct((2, *near.shape), near.dtype),
            jax.ShapeDtypeStruct((2, *far.shape), far.dtype),
        ),
        in_specs=[WHOLE] * 3 + [ANY] * 4,
        out_specs=[ANY] * 9,
        scratch_shapes=[
            dma((kinds,)), dma((kinds,)),
            dma((peers - 1, kinds)), dma((peers - 1, kinds)),
            dma((2, 2 * planes, 2)), dma((2, 2 * planes, 2)),
            dma((2,)), dma((2,)),
            dma((2, 4 * planes)), dma((2, 4 * planes)),
            dma((2, 4 * planes, 2)), dma((2, 4 * planes, 2)),
            dma((3, kinds)), dma((3, kinds)),
            dma((2 + kinds,)),
        ],
        compiler_params=pltpu.CompilerParams(
            collective_id=0, has_side_effects=True, vmem_limit_bytes=24 << 20
        ),
        name="spread",
    )(weights, tokens, upstream, far, near, *others)


def add_rows(target, left, right, step=256):
    def some(number, carry):
        here = pl.ds(pl.multiple_of(number * step, step), step)
        total = left[here, :].astype(jnp.float32) + right[here, :].astype(jnp.float32)
        target[here, :] = total.astype(target.dtype)
        return carry

    lax.fori_loop(0, target.shape[0] // step, some, 0)


class Grads:
    def __init__(self, peers, width, packed, arrived, send, recv, own_sem):
        self.peers, self.width, self.packed, self.arrived = peers, width, packed, arrived
        self.send, self.recv, self.own_sem = send, recv, own_sem
        self.me = lax.axis_index("dp")
        self.kinds = arrived.shape[0]

    def place(self, dp, kind):
        return self.arrived.at[kind, :, pl.ds(first_column(dp, self.width), self.width)]

    def rows(self, peer, kind):
        return self.packed.at[peer, :, pl.ds(kind * self.width, self.width)]

    def out(self, off, kind):
        peer = (self.me + off) % self.peers
        return remote(
            self.rows(peer, kind), self.place(self.me, kind),
            self.send.at[off - 1, kind], self.recv.at[off - 1, kind], dp=peer,
        )

    def into(self, off, kind):
        peer = (self.me + self.peers - off) % self.peers
        here = self.place(peer, kind)
        return remote(
            here, here, self.send.at[off - 1, kind], self.recv.at[off - 1, kind], dp=peer
        )

    def own(self, kind):
        return pltpu.make_async_copy(
            self.rows(self.me, kind), self.place(self.me, kind), self.own_sem.at[kind]
        )

    def start(self):
        @pl.when(self.me != IDLE)
        def _():
            for off in sorted(range(1, self.peers), key=lambda off: abs(2 * off - self.peers)):
                for kind in range(self.kinds):
                    self.out(off, kind).start()
            for kind in range(self.kinds):
                self.own(kind).start()

    def wait(self):
        for off in range(1, self.peers):
            @pl.when((self.me + self.peers - off) % self.peers != IDLE)
            def _():
                for kind in range(self.kinds):
                    self.into(off, kind).wait_recv()

        @pl.when(self.me != IDLE)
        def _():
            for off in range(1, self.peers):
                for kind in range(self.kinds):
                    self.out(off, kind).wait_send()
            for kind in range(self.kinds):
                self.own(kind).wait()


def swap_sum_kernel(scale, peers, width, packed, hidden, down, arrived, shares, send, recv,
                    own_sem, partial, from_core, both_cores, from_chip, c_send, c_recv, x_send, x_recv):
    unit = lax.axis_index("mp")
    core, chip = other_core(unit), other_chip(unit)
    grads = Grads(peers, width, packed, arrived, send, recv, own_sem)
    share = partial.shape[1] // 4
    greet(peers)

    def columns(unit):
        return partial.at[:, pl.ds(pl.multiple_of(unit * share, share), share)]

    def to_core(far):
        whose = other_chip(core) if far else core
        return remote(
            columns(whose), from_core.at[far], c_send.at[far], c_recv.at[far], mp=core
        )

    def multiply(unit, step=256):
        first = pl.multiple_of(unit * share, share)
        features = down[pl.ds(first, share), :]

        def some(number, carry):
            here = pl.ds(pl.multiple_of(number * step, step), step)
            value = lax.dot_general(
                hidden[here, :], features, (((1,), (1,)), ((), ())),
                preferred_element_type=jnp.float32,
            )
            partial[here, pl.ds(first, share)] = (value * scale).astype(partial.dtype)
            return carry

        lax.fori_loop(0, partial.shape[0] // step, some, 0)

    across = remote(both_cores, from_chip, x_send, x_recv, mp=chip)
    grads.start()
    multiply(other_chip(core))
    multiply(core)
    to_core(1).start()
    multiply(chip)
    to_core(0).start()
    multiply(unit)
    to_core(1).wait_recv()
    add_rows(both_cores, columns(chip), from_core.at[1])
    to_core(0).wait_recv()
    across.start()
    add_rows(from_core.at[0], columns(unit), from_core.at[0])
    across.wait_recv()
    add_rows(shares, from_core.at[0], from_chip)
    across.wait_send()
    for far in (1, 0):
        to_core(far).wait_send()
    grads.wait()


def swap_shares_kernel(peers, width, packed, shares, arrived, gathered, send, recv, own_sem,
                       from_beside, both, y_send, y_recv, z_send, z_recv, keep_sem):
    me = lax.axis_index("dp")
    z, y = me // 2, me % 2
    planes = peers // 2
    grads = Grads(peers, width, packed, arrived, send, recv, own_sem)
    group = shares.shape[0] // peers
    barrier = pltpu.get_barrier_semaphore()
    for off in range(1, peers):
        pl.semaphore_signal(
            barrier,
            inc=1,
            device_id={"dp": (me + off) % peers},
            device_id_type=pl.DeviceIdType.MESH,
        )
    pl.semaphore_wait(barrier, peers - 1)

    def rows(dp):
        return shares.at[pl.ds(pl.multiple_of(dp * group, group), group)]

    def along_y(plane):
        return remote(
            rows(plane * 2 + 1 - y), from_beside.at[plane],
            y_send.at[plane], y_recv.at[plane], dp=z * 2 + 1 - y,
        )

    def along_z(by):
        plane = (z + by) % planes
        return remote(
            both.at[plane], gathered.at[z], z_send.at[by - 1], z_recv.at[by - 1],
            dp=plane * 2 + y,
        )

    def along_z_in(by):
        plane = (z + planes - by) % planes
        here = gathered.at[plane]
        return remote(
            here, here, z_send.at[by - 1], z_recv.at[by - 1], dp=plane * 2 + y
        )

    for plane in range(planes):
        along_y(plane).start()
    grads.start()
    for plane in range(planes):
        along_y(plane).wait_recv()
        add_rows(both.at[plane], rows(plane * 2 + y), from_beside.at[plane])
    keep = pltpu.make_async_copy(both.at[z], gathered.at[z], keep_sem)
    for plane in range(planes):
        along_y(plane).wait_send()
    for by in range(1, planes):
        along_z(by).start()
    keep.start()
    for by in range(1, planes):
        along_z_in(by).wait_recv()
        along_z(by).wait_send()
    keep.wait()
    grads.wait()


def swap(kernel, packed, columns, kinds, others, gives, more, collective_id):
    peers, rows, across = packed.shape
    dma = pltpu.SemaphoreType.DMA
    return pl.pallas_call(
        functools.partial(kernel, peers, across // kinds),
        out_shape=[
            jax.ShapeDtypeStruct((kinds, rows, columns), packed.dtype),
            jax.ShapeDtypeStruct(gives, packed.dtype),
        ],
        in_specs=[WHOLE] * (1 + len(others)),
        out_specs=[ANY, WHOLE],
        scratch_shapes=[dma((peers - 1, kinds)), dma((peers - 1, kinds)), dma((kinds,)), *more],
        compiler_params=pltpu.CompilerParams(
            collective_id=collective_id, has_side_effects=True, vmem_limit_bytes=40 << 20
        ),
        name="swap",
    )(packed, *others)


def swap_sum(packed, columns, kinds, hidden, down, scale):
    rows, features = hidden.shape[0], down.shape[0]
    share = (rows, features // 4)
    dma = pltpu.SemaphoreType.DMA
    more = [
        pltpu.VMEM((rows, features), packed.dtype),
        pltpu.VMEM((2, *share), packed.dtype),
        pltpu.VMEM(share, packed.dtype),
        pltpu.VMEM(share, packed.dtype),
        dma((2,)), dma((2,)), dma, dma,
    ]
    kernel = functools.partial(swap_sum_kernel, scale)
    return swap(kernel, packed, columns, kinds, (hidden, down), share, more, 1)


def swap_shares(packed, columns, kinds, shares):
    peers = packed.shape[0]
    planes = peers // 2
    landed = (planes, shares.shape[0] // peers, shares.shape[1])
    dma = pltpu.SemaphoreType.DMA
    more = [pltpu.VMEM(landed, shares.dtype)] * 2
    more += [dma((planes,)), dma((planes,)), dma((planes - 1,)), dma((planes - 1,)), dma]
    return swap(swap_shares_kernel, packed, columns, kinds, (shares,), landed, more, 2)


STEP_ROWS = 72
STEP_COLUMNS = 896


def shifted(ref, which, start, cols):
    wide = STEP_ROWS + 8
    down = start % 8
    rows = ref[which, pl.ds(pl.multiple_of(start - down, 8), wide), cols]
    rows = pltpu.roll(rows.reshape(wide // 8, 8, rows.shape[1]), 8 - down, 1)
    inside = lax.broadcasted_iota(jnp.int32, rows[1:].shape, 1) < 8 - down
    return jnp.where(inside, rows[:-1], rows[1:]).reshape(STEP_ROWS, rows.shape[2])


def adam_kernel(numbers, *refs):
    owns, nears, straights, relays = refs[:3], refs[3:5], refs[5:7], refs[7:9]
    grads, last_grads, outs = *refs[9:11], refs[11:14]
    from_own, from_left = refs[14:]
    arrived, left_skip, count, odd = numbers[0], numbers[1], numbers[2], numbers[3]
    capacity_old = owns[0].shape[1]
    capacity_new = outs[0].shape[1]
    half = nears[0].shape[1]

    def state(pair, which):
        return pair[1][which - 1, 0] if which else pair[0][0]

    for which in range(3):
        from_own[which, pl.ds(capacity_new, capacity_old), :] = owns[which][0]
        from_left[which, pl.ds(0, half), :] = state(nears, which).astype(jnp.float32)
        far = pl.ds(half, capacity_old - half)

        @pl.when(odd > 0)
        def _():
            from_left[which, far, :] = state(straights, which).astype(jnp.float32)

        @pl.when(odd == 0)
        def _():
            from_left[which, far, :] = state(relays, which).astype(jnp.float32)

    kinds = pl.num_programs(0)
    is_last = pl.program_id(0) == kinds - 1

    pieces = outs[0].shape[2] // STEP_COLUMNS

    def some_rows(step, carry):
        first = pl.multiple_of(step // pieces * STEP_ROWS, 8)
        here = pl.ds(first, STEP_ROWS)
        cols = pl.ds(pl.multiple_of(step % pieces * STEP_COLUMNS, 128), STEP_COLUMNS)
        slot = first + lax.broadcasted_iota(jnp.int32, (STEP_ROWS, STEP_COLUMNS), 0)

        def finish(rows):
            grad = jnp.where(is_last, last_grads[0, here, cols], grads[0, here, cols])
            updated = adam_step(rows[0], rows[1], rows[2], grad.astype(jnp.float32))
            for which in range(3):
                outs[which][0, here, cols] = jnp.where(slot < count, updated[which], 0.0)

        own = first + capacity_new - arrived

        @pl.when(first < arrived)
        def _():
            finish([
                jnp.where(
                    slot < arrived,
                    shifted(from_left, which, first + left_skip, cols),
                    shifted(from_own, which, own, cols),
                )
                for which in range(3)
            ])

        @pl.when(first >= arrived)
        def _():
            finish([shifted(from_own, which, own, cols) for which in range(3)])

        return carry

    lax.fori_loop(0, capacity_new // STEP_ROWS * pieces, some_rows, 0)


def adam(states, moved, grads, last_grads, numbers):
    kinds, capacity_old, columns = states[0].shape
    capacity_new = grads.shape[1]
    width = columns // 2 if columns % 256 == 0 else columns

    def block(rows):
        return pl.BlockSpec((1, rows, width), lambda kind, part, _: (kind, 0, part))

    def given(value, parity):
        def used(numbers):
            return 1 if parity is None else 1 - (numbers[3] - parity) * (numbers[3] - parity)

        if value.ndim == 3:
            shape = (1, value.shape[1], width)
            return pl.BlockSpec(shape, lambda kind, part, n: (kind * used(n), 0, part * used(n)))
        shape = (2, 1, value.shape[2], width)
        return pl.BlockSpec(shape, lambda kind, part, n: (0, kind * used(n), 0, part * used(n)))

    first_grads = pl.BlockSpec(
        (1, capacity_new, width), lambda kind, part, _: (jnp.minimum(kind, kinds - 2), 0, part)
    )
    third_grads = pl.BlockSpec((1, capacity_new, width), lambda kind, part, _: (0, 0, part))
    return pl.pallas_call(
        adam_kernel,
        out_shape=[jax.ShapeDtypeStruct((kinds, capacity_new, columns), jnp.float32)] * 3,
        grid_spec=pltpu.PrefetchScalarGridSpec(
            num_scalar_prefetch=1,
            grid=(kinds, columns // width),
            in_specs=[block(capacity_old)] * 3
            + [given(value, parity) for pair, parity in zip(moved, (None, 1, 0)) for value in pair]
            + [first_grads, third_grads],
            out_specs=[block(capacity_new)] * 3,
            scratch_shapes=[
                pltpu.VMEM((3, 2 * capacity_new + 8, width), jnp.float32),
                pltpu.VMEM((3, capacity_new + capacity_old + 8, width), jnp.float32),
            ],
        ),
        compiler_params=pltpu.CompilerParams(vmem_limit_bytes=60 << 20),
        name="adam",
    )(numbers, *states, *(value for pair in moved for value in pair), grads, last_grads)


def cast_kernel(own, near, far, weights):
    half = near.shape[1]
    near[0] = own[0, :half, :].astype(near.dtype)
    far[0] = own[0, half:, :].astype(far.dtype)
    weights[0] = own[0].astype(weights.dtype)


def cast(state):
    kinds, rows, columns = state.shape
    width = columns // 2 if columns % 256 == 0 else columns
    half = (rows + 15) // 16 * 8
    counts = (half, rows - half, rows)

    def block(count):
        return pl.BlockSpec((1, count, width), lambda kind, part: (kind, 0, part))

    return pl.pallas_call(
        cast_kernel,
        out_shape=[
            jax.ShapeDtypeStruct((kinds, count, columns), jnp.bfloat16) for count in counts
        ],
        grid=(kinds, columns // width),
        in_specs=[block(rows)],
        out_specs=[block(count) for count in counts],
        compiler_params=pltpu.CompilerParams(vmem_limit_bytes=32 << 20),
        name="cast",
    )(state)


def unpack_kernel(numbers, block, *refs):
    rows, laid = refs[:-1], refs[-1]
    owner = pl.program_id(0)
    owners = pl.num_programs(0)
    busy = numbers[owners + 1]
    start = numbers[owner]
    count = (numbers[owner + 1] - start) * busy
    shift = start % 16
    slots, width = block.shape[1], rows[0].shape[1]
    window = (slots + 30) // 16 * 16

    @pl.when(owner == 0)
    def _():
        laid[...] = jnp.zeros_like(laid)

    slot = lax.broadcasted_iota(jnp.int32, block.shape[1:], 0)
    values = jnp.where(slot < count, block[0], jnp.zeros_like(block[0]))
    place = lax.broadcasted_iota(jnp.int32, (window, slots), 0) - shift
    wanted = place == lax.broadcasted_iota(jnp.int32, (window, slots), 1)
    found = jnp.dot(
        wanted.astype(jnp.bfloat16), values, preferred_element_type=jnp.float32
    ).astype(jnp.bfloat16)
    here = pl.ds(pl.multiple_of(start - shift, 16), window)
    laid[here, :] = laid[here, :] + found

    @pl.when(owner == owners - 1)
    def _():
        for kind, row in enumerate(rows):
            row[...] = laid[: row.shape[0], kind * width : (kind + 1) * width]


def unpack(blocks, offsets, busy, features, kinds):
    owners, slots, across = blocks.shape
    width = across // kinds
    whole = pl.BlockSpec((features, width), lambda owner, _: (0, 0))
    return pl.pallas_call(
        unpack_kernel,
        out_shape=[jax.ShapeDtypeStruct((features, width), blocks.dtype)] * kinds,
        grid_spec=pltpu.PrefetchScalarGridSpec(
            num_scalar_prefetch=1,
            grid=(owners,),
            in_specs=[pl.BlockSpec((1, slots, across), lambda owner, _: (owner, 0, 0))],
            out_specs=[whole] * kinds,
            scratch_shapes=[pltpu.VMEM((features + slots + 24, across), blocks.dtype)],
        ),
        compiler_params=pltpu.CompilerParams(vmem_limit_bytes=24 << 20),
        name="unpack",
    )(jnp.concatenate([offsets, busy.astype(jnp.int32)[None]]), blocks)


def pack_kernel(offsets, *refs):
    grads, packed = refs[:-1], refs[-1]
    features, width = grads[0].shape
    slots = packed.shape[1]
    window = (slots + 30) // 16 * 16
    owner = pl.program_id(0)
    start = offsets[owner]
    count = offsets[owner + 1] - start
    first = jnp.minimum(start - start % 16, features - window)
    slot = lax.broadcasted_iota(jnp.int32, (slots, window), 0)
    place = lax.broadcasted_iota(jnp.int32, (slots, window), 1)
    wanted = ((place - slot == start - first) & (slot < count)).astype(jnp.bfloat16)
    for kind, grad in enumerate(grads):
        found = jnp.dot(
            wanted,
            grad[pl.ds(pl.multiple_of(first, 16), window), :],
            preferred_element_type=jnp.float32,
        )
        packed[0, :, kind * width : (kind + 1) * width] = found.astype(packed.dtype)


def pack(grads, offsets, slots):
    features, width = grads[0].shape
    owners = offsets.shape[0] - 1
    across = len(grads) * width
    whole = pl.BlockSpec((features, width), lambda owner, _: (0, 0))
    return pl.pallas_call(
        pack_kernel,
        out_shape=jax.ShapeDtypeStruct((owners, slots, across), grads[0].dtype),
        grid_spec=pltpu.PrefetchScalarGridSpec(
            num_scalar_prefetch=1,
            grid=(owners,),
            in_specs=[whole] * len(grads),
            out_specs=pl.BlockSpec((1, slots, across), lambda owner, _: (owner, 0, 0)),
        ),
        compiler_params=pltpu.CompilerParams(vmem_limit_bytes=24 << 20),
        name="pack",
    )(offsets, *grads)


def lane_split(columns, peers):
    return -(-columns // (peers * 128)) * 128


def product(left, right, left_dim, right_dim):
    return lax.dot_general(
        left,
        right,
        (((left_dim,), (right_dim,)), ((), ())),
        preferred_element_type=jnp.float32,
    )


def token_pass(tokens, upstream, casts, others, old_offsets, new_offsets, capacity_new):
    peers = lax.axis_size("dp")
    feature_peers = lax.axis_size("mp")
    near, far, weights = casts
    kinds, _, columns = weights.shape
    width = lane_split(columns, peers)
    features = tokens.shape[1]
    scale_in = features ** (-0.5)
    scale_hidden = (columns * feature_peers) ** (-0.5)
    busy = lax.axis_index("dp") != IDLE

    blocks, all_tokens, all_upstream, *arrived = spread(
        weights, tokens, upstream, far, near, others, peers, width
    )
    rows = unpack(blocks, old_offsets, busy, features, kinds)

    gate_act = product(all_tokens, rows[0], 1, 0) * scale_in
    up_act = product(all_tokens, rows[1], 1, 0) * scale_in
    back_grad = product(all_upstream, rows[2], 1, 0) * scale_hidden
    sigmoid_gate = jax.nn.sigmoid(gate_act)
    hidden = (gate_act * sigmoid_gate * up_act).astype(jnp.bfloat16)
    gate_grad = (
        back_grad * up_act * sigmoid_gate * (1.0 + gate_act * (1.0 - sigmoid_gate))
    ).astype(jnp.bfloat16)
    up_grad = (back_grad * gate_act * sigmoid_gate).astype(jnp.bfloat16)
    gate_grad, up_grad = lax.optimization_barrier((gate_grad, up_grad))

    grads = [
        (product(all_tokens, gate_grad, 0, 0) * scale_in).astype(jnp.bfloat16),
        (product(all_tokens, up_grad, 0, 0) * scale_in).astype(jnp.bfloat16),
    ]
    last_grads = (product(all_upstream, hidden, 0, 0) * scale_hidden).astype(jnp.bfloat16)
    first_packed = pack(grads, new_offsets, capacity_new)
    last_packed = pack([last_grads], new_offsets, capacity_new)
    grads, shares = swap_sum(first_packed, columns, kinds - 1, hidden, rows[2], scale_hidden)
    last_grads, shares = swap_shares(last_packed, columns, 1, shares)
    layer_output = jnp.sum(shares.astype(jnp.float32), axis=0).astype(jnp.bfloat16)
    return grads, last_grads, layer_output, arrived


def token_body(*arguments):
    return token_step(*arguments)


def token_step(tokens, out_grad, master, moment_one, moment_two, old_offsets, new_offsets):
    devices = lax.axis_size("dp")
    capacity_old = master.shape[0]
    capacity_new = new_capacity(tokens.shape[1], devices)
    device_index = lax.axis_index("dp")
    new_start = lookup(new_offsets, device_index)
    new_end = lookup(new_offsets, device_index + 1)
    old_start = lookup(old_offsets, device_index)
    left_start = lookup(old_offsets, jnp.maximum(device_index - 1, 0))
    live_flag = new_end != new_start
    upstream = jnp.where(live_flag, out_grad, jnp.zeros_like(out_grad))

    states = [value.transpose(1, 0, 2) for value in (master, moment_one, moment_two)]
    casts = cast(states[0])
    near = casts[0]
    grads, last_grads, layer_output, landed = token_pass(
        tokens, upstream, casts, states[1:], old_offsets, new_offsets, capacity_new
    )
    straight, straight_rest, hopped, relayed, near_rest, _ = landed
    near_rest = lax.ppermute(near_rest, "dp", [(i, i + 1) for i in range(devices - 1)])
    pairs = [(i, i + 1 - 2 * (i % 2)) for i in range(devices) if i != 1]
    near = lax.ppermute(jnp.where(device_index % 2 > 0, hopped, near), "dp", pairs)
    pairs = [(i, i + 2) for i in range(0, devices - 2, 2)]
    relayed_rest = lax.ppermute(straight_rest, "dp", pairs)
    moved = ((near, near_rest), (straight, straight_rest), (relayed, relayed_rest))
    arrived = jnp.clip(old_start - new_start, 0, capacity_new)
    left_skip = jnp.clip(new_start - left_start, 0, capacity_old)
    numbers = jnp.stack([arrived, left_skip, new_end - new_start, device_index % 2])
    updated = adam(states, moved, grads, last_grads, numbers)
    updated = [value.transpose(1, 0, 2) for value in updated]
    layer_output = jnp.where(live_flag, layer_output, jnp.zeros_like(layer_output))
    return (updated[0], updated[1], updated[2], layer_output)


def new_capacity(features, devices):
    shard_rows = features // devices
    jitter_rows = shard_rows // (2 * (devices - 1)) + 2
    return shard_rows + shard_rows // 4 + 2 * jitter_rows


def any_body(tokens, out_grad, master, *others):
    devices = lax.axis_size("dp")
    columns = master.shape[2]
    moved_tokens = 3 * tokens.shape[0] * devices
    moved_rows = 2 * master.shape[1] * columns
    whole = (
        devices % 2 == 0
        and lax.axis_size("mp") == 4
        and tokens.shape[0] % 64 == 0
        and columns == (devices - 1) * lane_split(columns, devices)
        and new_capacity(tokens.shape[1], devices) % STEP_ROWS == 0
        and columns % (2 * STEP_COLUMNS) == 0
    )
    chosen = token_body if whole and moved_tokens <= moved_rows else body
    return chosen(tokens, out_grad, master, *others)


def solution(mesh):
    placed = (
        P("dp", None),
        P("dp", None),
        P("dp", None, "mp"),
        P("dp", None, "mp"),
        P("dp", None, "mp"),
        P(),
        P(),
    )
    return jax.shard_map(
        any_body,
        mesh=mesh,
        in_specs=placed,
        out_specs=(P("dp", None, "mp"), P("dp", None, "mp"), P("dp", None, "mp"), P("dp", "mp")),
        check_vma=False,
    )
```
